1024 devices in a mesh: lev: 16 (over y, core), lat: 64 (over x, z).
Axes of the slice: x: 8, y: 8, z: 8, core: 2. Of those that a mesh axis runs over, the one named last changes fastest.
Arguments:
- humidity: bfloat16 [64, 128, 2560], P('lev', 'lat'), may hold values from -6 to 6
- wind_east: bfloat16 [64, 128, 2560], P('lev', 'lat'), may hold values from -6 to 6
- wind_north: bfloat16 [64, 128, 2560], P('lev', 'lat'), may hold values from -6 to 6
- legendre: bfloat16 [640, 640, 128], P('lat'), may hold values from -0.5 to 0.5
- owner: int32 [640], replicated, may hold values from 0 to 63, as said below
- vertical_modes: float32 [64, 64], replicated, may hold values from -1 to 1, as said below
- mode_values: float32 [64], replicated, may hold values from 0.2 to 2
Outputs:
- spectral: float32 [640, 640, 384], P('lat', 'lev')
The draws below stay inside these ranges and needn't reach their ends.
Inputs may be any that keep to these rules, and one draw needn't show every extreme that they name: Every owner is named by exactly 10 wavenumbers, and wavenumbers m and 639 - m have the same owner. `vertical_modes`: an orthogonal matrix.
All inputs are finite; a program needn't handle non-finite values.
Results may differ from the reference program's by a relative error of at most 0.0048.
Values may be sent and summed in bfloat16 or wider, within the bound.
A program may use at most 64 MiB of HBM per device.

```python
import math
import jax
import jax.numpy as jnp
from jax import lax

TRUNC = 640
NLON = 2560
LEV = 64
NLAT = 128
N_LAT = 64


def draw_owner(key, part):
    half_count = TRUNC // 2
    pairs_each = TRUNC // N_LAT // 2
    shuffled = jax.random.permutation(key, half_count).astype(jnp.int32)
    pair_owner = shuffled // pairs_each
    waves = jnp.arange(TRUNC, dtype=jnp.int32)
    return pair_owner[jnp.minimum(waves, TRUNC - 1 - waves)]


def draw_vertical_modes(key, part):
    key_modes = jax.random.fold_in(key, 31)
    return jax.random.orthogonal(key_modes, LEV, dtype=jnp.float32)


def levels(rng, dims, split, smallest, high):
    loudness, own = 1.0, jax.random.fold_in(rng, 6)
    for position, shards_of in split:
        draws = jnp.exp(jax.random.uniform(jax.random.fold_in(own, position), (shards_of,), jnp.float32, smallest / len(split), high / len(split)))
        loudness = loudness * jnp.repeat(draws, dims[position] // shards_of).reshape([-1 if axis == position else 1 for axis in range(len(dims))])
    return loudness


def bell_draw(stream_key, extent, scale, reach, split=(), kind=jnp.bfloat16):
    values = jax.random.normal(stream_key, extent, jnp.float32) * scale
    if len(split) > 0:
        values = levels(stream_key, extent, split, -0.22, 0.18) * values
    return jnp.clip(values, min=-reach, max=reach).astype(kind)


def setup_inputs(seed: int = 0) -> dict:
    key_list = jax.random.split(jax.random.key(seed), 8)
    return {
        "humidity": bell_draw(key_list[0], (LEV, NLAT, NLON), 1.0, 6.0, ((0, 16), (1, 64))),
        "wind_east": bell_draw(key_list[1], (LEV, NLAT, NLON), 1.0, 6.0, ((0, 16), (1, 64))),
        "wind_north": bell_draw(key_list[2], (LEV, NLAT, NLON), 1.0, 6.0, ((0, 16), (1, 64))),
        "legendre": bell_draw(key_list[3], (TRUNC, TRUNC, NLAT), NLAT ** -0.5, 0.5, ((0, 64),)),
        "owner": draw_owner(jax.random.fold_in(key_list[7], 71), 0),
        "vertical_modes": draw_vertical_modes(jax.random.fold_in(key_list[7], 71), 0),
        "mode_values": jnp.clip(jnp.exp(jax.random.uniform(key_list[6], (LEV,), jnp.float32, math.log(0.2), math.log(2.0))), 0.2, 2.0),
    }


def make_twiddle(waves, lon_count):
    longitude = jnp.arange(lon_count, dtype=jnp.int32)
    phase = waves[:, None] * longitude[None, :] % lon_count
    angle = phase.astype(jnp.float32) * (2.0 * math.pi / lon_count)
    factor = 1.0 / math.sqrt(lon_count)
    table = jnp.stack([jnp.cos(angle) * factor, -jnp.sin(angle) * factor], axis=1).astype(jnp.bfloat16)
    return table.reshape(-1, lon_count)

def reference(humidity, wind_east, wind_north, legendre, owner, vertical_modes, mode_values):
    waves = jnp.arange(TRUNC, dtype=jnp.int32)
    order = jnp.argsort(owner * TRUNC + waves, stable=True).astype(jnp.int32)
    twiddle = make_twiddle(order, NLON).astype(jnp.float32)

    def one_level(fields):
        moist, east, north = fields
        flux_east = (east.astype(jnp.float32) * moist.astype(jnp.float32)).astype(jnp.bfloat16)
        flux_north = (north.astype(jnp.float32) * moist.astype(jnp.float32)).astype(jnp.bfloat16)
        grid_rows = jnp.stack([moist, flux_east, flux_north]).reshape(3 * NLAT, NLON).astype(jnp.float32)
        fourier = jnp.dot(twiddle, grid_rows.T, precision=lax.Precision.HIGHEST)
        return fourier.astype(jnp.bfloat16).reshape(TRUNC, 2, 3, NLAT)
    fourier = lax.map(one_level, (humidity, wind_east, wind_north))
    fourier = fourier.transpose(1, 2, 3, 0, 4).reshape(TRUNC, 6 * LEV, NLAT)
    degree = waves.astype(jnp.float32)
    shift = 4.0 * degree * (degree + 1.0) / (TRUNC * TRUNC)
    inverse = 1.0 / (1.0 + shift[:, None] * mode_values[None, :])

    def project(items):
        table_block, fourier_block, wave_block = items
        live = waves[None, :, None] >= wave_block[:, None, None]
        masked = jnp.where(live, table_block.astype(jnp.float32), 0.0)
        projected = jnp.einsum('snk,syk->sny', masked, fourier_block.astype(jnp.float32), precision=lax.Precision.HIGHEST)
        projected = projected.reshape(projected.shape[0], TRUNC, 6, LEV)
        modal = jnp.einsum('snyj,jk->snyk', projected, vertical_modes, precision=lax.Precision.HIGHEST)
        modal = modal * inverse[None, :, None, :]
        solved = jnp.einsum('snyk,lk->snyl', modal, vertical_modes, precision=lax.Precision.HIGHEST)
        return solved.reshape(solved.shape[0], TRUNC, 6 * LEV)
    width = 32
    spectral = lax.map(project, (legendre.reshape(TRUNC // width, width, TRUNC, NLAT), fourier.reshape(TRUNC // width, width, 6 * LEV, NLAT), order.reshape(TRUNC // width, width)))
    return spectral.reshape(TRUNC, TRUNC, 6 * LEV)
```

```python
import functools
import math

import jax
import jax.numpy as jnp
import numpy as np
from jax import lax
from jax.experimental import pallas as pl
from jax.experimental.pallas import tpu as pltpu
from jax.sharding import PartitionSpec as P

MESH = pl.DeviceIdType.MESH
F32, BF16 = jnp.float32, jnp.bfloat16
RADIX = 20
CORES = 2


def split_lat(count):
    side = 1 << (int(math.log2(count)) // 2)
    return count // side, side


def lane_waves(units):
    rows = []
    for c in range(RADIX // 2):
        first, second = (0, RADIX // 2) if c == 0 else (c, RADIX - c)
        rows += [RADIX * u + first for u in range(units)] + [RADIX * u + second for u in range(units)]
    return np.array(rows)


def fourier_table(lon, units):
    inner = lon // RADIX
    waves = lane_waves(units).reshape(RADIX // 4, 4 * units)
    flip = np.ones((RADIX // 2, 2, units))
    flip[1:, 1] = -1.0
    flip = flip.reshape(RADIX // 4, 4 * units)
    phase = waves[:, None, :] * np.arange(inner)[None, :, None] % lon
    cos = np.cos(2 * np.pi * phase / lon) / math.sqrt(lon)
    sin = np.sin(2 * np.pi * phase / lon) / math.sqrt(lon)
    flip = flip[:, None, :]
    top = np.concatenate([cos, -sin], axis=2)
    bottom = np.concatenate([sin * flip, cos * flip], axis=2)
    return np.concatenate([top, bottom], axis=1)


def dot(a, b, contract=(1, 0)):
    return lax.dot_general(
        a, b, (((contract[0],), (contract[1],)), ((), ())), preferred_element_type=F32
    )


def iota(shape, axis):
    return lax.broadcasted_iota(jnp.int32, shape, axis)


def floor_div(value, divisor):
    return jnp.floor((value.astype(F32) + 0.5) * (1.0 / divisor))


def one_hot(mask):
    return jnp.where(mask, 1.0, 0.0).astype(BF16)


def short_fourier(x, inner):
    part = [x[:, inner * h : inner * (h + 1)] for h in range(RADIX)]
    half = RADIX // 2
    even = [part[h] + part[RADIX - h] for h in range(1, half)]
    odd = [part[h] - part[RADIX - h] for h in range(1, half)]
    real, imag = [None] * (half + 1), [None] * (half + 1)
    for q in range(half // 2 + 1):
        sums = []
        for parity in (0, 1):
            total = None
            for h in range(1, half):
                if h % 2 == parity:
                    factor = math.cos(2 * math.pi * ((q * h) % RADIX) / RADIX)
                    term = even[h - 1] * factor
                    total = term if total is None else total + term
            sums.append(total)
        ends_plus, ends_minus = part[0] + part[half], part[0] - part[half]
        first = sums[0] + (ends_plus if q % 2 == 0 else ends_minus)
        real[q] = first + sums[1]
        if q != half - q:
            other = sums[0] + (ends_plus if (half - q) % 2 == 0 else ends_minus)
            real[half - q] = other - sums[1]
    for q in range(half // 2 + 1):
        sums = []
        for parity in (0, 1):
            total = None
            for h in range(1, half):
                if h % 2 == parity:
                    factor = -math.sin(2 * math.pi * ((q * h) % RADIX) / RADIX)
                    term = odd[h - 1] * factor
                    total = term if total is None else total + term
            sums.append(total)
        imag[q] = sums[0] + sums[1]
        if q != half - q:
            imag[half - q] = sums[1] - sums[0]
    return real, imag


def kernel(
    cfg, hum_ref, east_ref, north_ref, leg_ref, owner_ref, modes_ref, values_ref, table_ref,
    out_ref,
    out_buf, x_buf, z_send, z_buf, y_buf, leg_raw, leg_buf, first_buf, last_buf, scale_buf, proj_buf,
    leg_sem, x_send, x_recv, z_send_sem, z_recv, up_send, up_recv, down_send, down_recv,
    side_send, side_recv,
):
    nx, nz, ny, slots, levels, trunc, lon, block = (
        cfg[k] for k in ("nx", "nz", "ny", "slots", "levels", "trunc", "lon", "block")
    )
    lev, lat = lax.axis_index("lev"), lax.axis_index("lat")
    x, z = lat // nz, lat % nz
    y, core = lev // CORES, lev % CORES
    inner, units = lon // RADIX, trunc // RADIX
    fields = 3
    piece = 2 * fields * levels
    rows = slots * piece
    width = out_buf.shape[1]
    lats = nx * nz * 2
    total_levels = ny * CORES * levels
    flat = 2 * fields * total_levels
    bundle = 2 * nz
    bundle_z = 2 * nx

    def along_x(i):
        return {"lat": ((x + i) % nx) * nz + z}

    def along_z(i):
        return {"lat": x * nz + (z + i) % nz}

    def along_y(i):
        return {"lev": ((y + i) % ny) * CORES + core}

    partner = {"lev": y * CORES + 1 - core}

    barrier = pltpu.get_barrier_semaphore()
    peers = [along_x(i) for i in range(1, nx)] + [along_z(i) for i in range(1, nz)]
    peers += [along_y(1), along_y(ny - 1), partner]
    for peer in peers:
        pl.semaphore_signal(barrier, inc=1, device_id=peer, device_id_type=MESH)

    leg_copy = pltpu.make_async_copy(
        leg_ref.at[:, pl.ds(pl.multiple_of(lev * block, 8), block), :], leg_raw, leg_sem
    )
    leg_copy.start()

    owner = owner_ref[...].astype(F32)
    owners = nx * nz
    member = owner == iota((owners, trunc), 0).astype(F32)
    before = one_hot(iota((trunc, trunc), 0) < iota((trunc, trunc), 1))
    count = dot(one_hot(member), before)
    rank = jnp.sum(jnp.where(member, count, 0.0), axis=0, keepdims=True)
    mine = (owner == lat.astype(F32)) & (rank == iota((16, trunc), 0).astype(F32))
    own_waves = jnp.sum(
        jnp.where(mine, iota((16, trunc), 1).astype(F32), 0.0), axis=1, keepdims=True
    )
    lane = iota((1, trunc), 1)
    clas = floor_div(lane, 2 * units)
    within = lane.astype(F32) - clas * (2 * units)
    second = within >= units
    unit = jnp.where(second, within - units, within)
    residue = jnp.where(second, jnp.where(clas == 0, RADIX // 2, RADIX - clas), clas)
    wave = RADIX * unit + residue
    reorder = one_hot(iota((trunc, trunc), 0).astype(F32) == wave)
    both = jnp.where(iota((16, trunc), 0) == 0, owner, jnp.where(iota((16, trunc), 0) == 1, rank, 0.0))
    both = dot(both.astype(BF16), reorder)
    owner_lane, rank_lane = both[0:1], both[1:2]

    humidity = hum_ref[...].astype(F32).reshape(2 * levels, lon)
    east = east_ref[...].astype(F32).reshape(2 * levels, lon)
    north = north_ref[...].astype(F32).reshape(2 * levels, lon)
    east = (east * humidity).astype(BF16).astype(F32)
    north = (north * humidity).astype(BF16).astype(F32)
    grid = jnp.concatenate([humidity, east, north], axis=0)
    real, imag = short_fourier(grid, inner)
    joined = [jnp.concatenate([r, i], axis=1) for r, i in zip(real, imag)]
    grid_rows = grid.shape[0]
    reals, imags = [], []
    for p in range(RADIX // 4):
        table = table_ref[p]
        if p == 0:
            left = jnp.concatenate([joined[0], joined[RADIX // 2], joined[1]], axis=0)
            limits = [units, 2 * units]
        else:
            left = jnp.concatenate([joined[2 * p], joined[2 * p + 1]], axis=0)
            limits = [2 * units]
        high = left.astype(BF16)
        low = (left - high.astype(F32)).astype(BF16)
        result = dot(high, table) + dot(low, table) + dot(high, table_ref[RADIX // 4 + p])
        column = iota((grid_rows, 8 * units), 1)
        column = jnp.where(column >= 4 * units, column - 4 * units, column)
        picked = result[len(limits) * grid_rows :]
        for k in reversed(range(len(limits))):
            picked = jnp.where(
                column < limits[k], result[k * grid_rows : (k + 1) * grid_rows], picked
            )
        reals.append(picked[:, : 4 * units])
        imags.append(picked[:, 4 * units :])
    spectrum = jnp.concatenate(
        [jnp.concatenate(reals, axis=1), jnp.concatenate(imags, axis=1)], axis=0
    ).astype(BF16)

    source = iota((piece, 2 * grid_rows), 1)
    target = iota((piece, 2 * grid_rows), 0)
    spread = []
    for t in range(2):
        pick = one_hot(2 * target + t == source)
        spread.append(dot(pick, spectrum))
    halves = []
    for t in range(2):
        pieces = [
            jnp.where(rank_lane == float(s), spread[t], 0.0) for s in range(slots)
        ] + [jnp.zeros((width - rows, trunc), F32)]
        halves.append(jnp.concatenate(pieces, axis=0))
    right = jnp.concatenate(halves, axis=1).astype(BF16)
    row = iota((2 * owners, trunc), 0).astype(F32)
    choose = jnp.concatenate(
        [
            jnp.where(2.0 * owner_lane == row, 1.0, 0.0),
            jnp.where(2.0 * owner_lane + 1.0 == row, 1.0, 0.0),
        ],
        axis=1,
    ).astype(BF16)
    out_buf[...] = dot(choose, right, (1, 1)).astype(BF16)

    pl.semaphore_wait(barrier, len(peers))

    copies = []
    for i in range(1, nx):
        to = (x + i) % nx
        copy = pltpu.make_async_remote_copy(
            src_ref=out_buf.at[pl.ds(pl.multiple_of(to * bundle, bundle), bundle)],
            dst_ref=x_buf.at[pl.ds(pl.multiple_of(x * bundle, bundle), bundle)],
            send_sem=x_send.at[i],
            recv_sem=x_recv.at[i],
            device_id=along_x(i),
            device_id_type=MESH,
        )
        copy.start()
        copies.append(copy)
    x_buf[pl.ds(pl.multiple_of(x * bundle, bundle), bundle), :] = out_buf[
        pl.ds(pl.multiple_of(x * bundle, bundle), bundle), :
    ]

    leg_copy.wait()
    arrive = iota((lats, lats), 1)
    from_z = arrive // bundle_z
    from_x = (arrive % bundle_z) // 2
    reach = one_hot(iota((lats, lats), 0) == (from_x * nz + from_z) * 2 + arrive % 2)
    leg = leg_raw[...].astype(F32).reshape(slots * block, lats).astype(BF16)
    leg = dot(leg, reach)
    degree = iota((block, lats), 0).astype(F32) + (lev * block).astype(F32)
    for s in range(slots):
        live = degree >= own_waves[s : s + 1, :]
        leg_buf[block * s : block * (s + 1), :] = jnp.where(
            live, leg[block * s : block * (s + 1)], 0.0
        )

    swap_to = iota((2 * owners, 2 * owners), 0)
    swap_from = iota((2 * owners, 2 * owners), 1)
    part_z, part_x, part_t = swap_to // bundle_z, (swap_to % bundle_z) // 2, swap_to % 2
    swap = one_hot(swap_from == part_x * bundle + part_z * 2 + part_t)

    for copy in copies:
        copy.wait_recv()
    z_send[...] = dot(swap, x_buf[...]).astype(BF16)
    copies_z = []
    for i in range(1, nz):
        to = (z + i) % nz
        copy = pltpu.make_async_remote_copy(
            src_ref=z_send.at[pl.ds(pl.multiple_of(to * bundle_z, bundle_z), bundle_z)],
            dst_ref=z_buf.at[pl.ds(pl.multiple_of(z * bundle_z, bundle_z), bundle_z)],
            send_sem=z_send_sem.at[i],
            recv_sem=z_recv.at[i],
            device_id=along_z(i),
            device_id_type=MESH,
        )
        copy.start()
        copies_z.append(copy)
    z_buf[pl.ds(pl.multiple_of(z * bundle_z, bundle_z), bundle_z), :] = z_send[
        pl.ds(pl.multiple_of(z * bundle_z, bundle_z), bundle_z), :
    ]

    modes = modes_ref[...]
    modes_high = modes.astype(BF16)
    modes_low = (modes - modes_high.astype(F32)).astype(BF16)
    tl = total_levels
    tile = one_hot(iota((tl, flat), 0) == (iota((tl, flat), 1) & (tl - 1)))
    column_part = iota((flat, flat), 1) // tl
    row_id = iota((flat, flat), 0)
    group = floor_div(row_id, piece)
    row_in = row_id.astype(F32) - group * piece
    row_part = floor_div(row_in, levels)
    id64 = iota((flat, tl), 0)
    group64 = floor_div(id64, piece)
    level64 = id64.astype(F32) - group64 * piece
    level64 = level64 - floor_div(level64, levels) * levels + levels * group64
    gather = one_hot(level64 == iota((flat, tl), 1).astype(F32))
    for k, part in enumerate((modes_high, modes_low)):
        wide = dot(part, tile).astype(BF16)
        first_buf[k] = jnp.where(
            row_part == column_part.astype(F32), dot(gather, wide), 0.0
        ).astype(BF16)
        tall = dot(tile, part, (0, 1)).astype(BF16)
        last_buf[k] = jnp.where(row_id // tl == column_part, dot(tall, tile), 0.0).astype(BF16)
    values = jnp.concatenate([values_ref[...]] * (2 * fields), axis=1)
    number = iota((block, flat), 0).astype(F32) + (lev * block).astype(F32)
    shift = 4.0 * number * (number + 1.0) / (trunc * trunc)
    scale_buf[...] = 1.0 / (1.0 + shift * values)

    for copy in copies_z:
        copy.wait_recv()
    own = z_buf[...].astype(F32).T
    y_buf[lev] = own[:rows].astype(BF16)

    chunks = cfg["chunks"]
    starts = [sum(chunks[:k]) for k in range(len(chunks))]
    half = len(chunks) // 2
    far = ny // 2
    pending = []

    def send(group_id, k, send_sem, recv_sem, to):
        view = y_buf.at[group_id, pl.ds(starts[k], chunks[k])]
        copy = pltpu.make_async_remote_copy(
            src_ref=view, dst_ref=view, send_sem=send_sem, recv_sem=recv_sem,
            device_id=to, device_id_type=MESH,
        )
        copy.start()
        pending.append(copy)

    def arrival(group_id, k, sem):
        view = y_buf.at[group_id, pl.ds(starts[k], chunks[k])]
        pltpu.make_async_remote_copy(
            src_ref=view, dst_ref=view, send_sem=sem, recv_sem=sem,
            device_id=partner, device_id_type=MESH,
        ).wait_recv()

    for k in range(len(chunks)):
        send(lev, k, up_send.at[0, k], up_recv.at[0, k], along_y(1))
        send(lev, k, down_send.at[0, k], down_recv.at[0, k], along_y(ny - 1))
    for k in range(len(chunks)):
        send(lev, k, side_send.at[0, k], side_recv.at[0, k], partner)
    for d in range(1, far + 1):
        below = ((y + ny - d) % ny) * CORES + core
        above = ((y + d) % ny) * CORES + core
        for k in range(len(chunks)):
            if d < far or k < half:
                arrival(below, k, up_recv.at[d - 1, k])
                if d < far - 1 or (d == far - 1 and k < half):
                    send(below, k, up_send.at[d, k], up_recv.at[d, k], along_y(1))
                send(below, k, side_send.at[d, k], side_recv.at[d, k], partner)
            if d < far or k >= half:
                arrival(above, k, down_recv.at[d - 1, k])
                if d < far - 1 or (d == far - 1 and k >= half):
                    send(above, k, down_send.at[d, k], down_recv.at[d, k], along_y(ny - 1))
                if d < far:
                    send(above, k, side_send.at[far + d, k], side_recv.at[far + d, k], partner)
                else:
                    send(above, k, side_send.at[d, k], side_recv.at[d, k], partner)
    other = 1 - core
    for d in range(far + 1):
        for k in range(len(chunks)):
            arrival(((y + ny - d) % ny) * CORES + other, k, side_recv.at[d, k])
            if 0 < d < far:
                arrival(((y + d) % ny) * CORES + other, k, side_recv.at[far + d, k])

    for s in range(slots):
        right = jnp.concatenate(
            [y_buf[g, piece * s : piece * (s + 1), :] for g in range(ny * CORES)], axis=0
        )
        left = leg_buf[block * s : block * (s + 1), :].astype(BF16)
        proj_buf[block * s : block * (s + 1), :] = dot(left, right, (1, 1))
    projected = proj_buf[...].astype(BF16)
    modal = dot(projected, first_buf[0]) + dot(projected, first_buf[1])
    scale = jnp.concatenate([scale_buf[...]] * slots, axis=0)
    modal = (modal * scale).astype(BF16)
    solved = dot(modal, last_buf[0]) + dot(modal, last_buf[1])
    out_ref[...] = solved.reshape(slots, block, flat)

    for copy in copies + copies_z + pending:
        copy.wait_send()


def build(nx, nz, ny, slots, levels, trunc, lon, chunks, width):
    block = trunc // (ny * CORES)
    rows = slots * 6 * levels
    flat = 6 * levels * ny * CORES
    lats = nx * nz * 2
    far = ny // 2
    cfg = dict(
        nx=nx, nz=nz, ny=ny, slots=slots, levels=levels, trunc=trunc, lon=lon, block=block,
        chunks=chunks,
    )
    dma = pltpu.SemaphoreType.DMA
    vmem = pl.BlockSpec(memory_space=pltpu.VMEM)
    hbm = pl.BlockSpec(memory_space=pl.ANY)
    nc = len(chunks)
    return pl.pallas_call(
        functools.partial(kernel, cfg),
        out_shape=jax.ShapeDtypeStruct((slots, block, flat), F32),
        in_specs=[vmem, vmem, vmem, hbm, vmem, vmem, vmem, vmem],
        out_specs=vmem,
        scratch_shapes=[
            pltpu.VMEM((lats, width), BF16),
            pltpu.VMEM((lats, width), BF16),
            pltpu.VMEM((lats, width), BF16),
            pltpu.VMEM((lats, width), BF16),
            pltpu.VMEM((ny * CORES, rows, lats), BF16),
            pltpu.VMEM((slots, block, lats), BF16),
            pltpu.VMEM((slots * block, lats), F32),
            pltpu.VMEM((2, flat, flat), BF16),
            pltpu.VMEM((2, flat, flat), BF16),
            pltpu.VMEM((block, flat), F32),
            pltpu.VMEM((slots * block, flat), F32),
            dma, dma((nx,)), dma((nx,)), dma((nz,)), dma((nz,)),
            dma((far, nc)), dma((far, nc)), dma((far, nc)), dma((far, nc)),
            dma((ny, nc)), dma((ny, nc)),
        ],
        compiler_params=pltpu.CompilerParams(
            collective_id=0, has_side_effects=True, vmem_limit_bytes=60 * 1024 * 1024
        ),
    )


def body(humidity, wind_east, wind_north, legendre, owner, vertical_modes, mode_values):
    trunc = owner.shape[0]
    levels, pair, lon = humidity.shape
    owners = lax.axis_size("lat")
    nx, nz = split_lat(owners)
    ny = lax.axis_size("lev") // CORES
    slots = legendre.shape[0]
    rows = slots * 6 * levels
    if rows % 16 == 0 and rows >= 64:
        quarter = -(-rows // 64) * 16
        chunks = [quarter] * 3 + [rows - 3 * quarter]
    else:
        chunks = [rows // 2, rows - rows // 2]
    width = -(-rows // 128) * 128
    table = fourier_table(lon, trunc // RADIX)
    high = table.astype(BF16)
    table = jnp.asarray(np.concatenate([high, (table - high.astype(np.float64)).astype(BF16)]))
    call = build(nx, nz, ny, slots, levels, trunc, lon, chunks, width)
    return call(
        humidity, wind_east, wind_north, legendre, owner.reshape(1, trunc), vertical_modes,
        mode_values.reshape(1, -1), table,
    )


def solution(mesh):
    return jax.shard_map(
        body,
        mesh=mesh,
        in_specs=(
            P("lev", "lat", None),
            P("lev", "lat", None),
            P("lev", "lat", None),
            P("lat", None, None),
            P(),
            P(),
            P(),
        ),
        out_specs=P("lat", "lev", None),
        check_vma=False,
    )
```

```python
import functools
import math

import jax
import jax.numpy as jnp
import numpy as np
from jax import lax
from jax.experimental import pallas as pl
from jax.experimental.pallas import tpu as pltpu
from jax.sharding import PartitionSpec as P

MESH = pl.DeviceIdType.MESH
F32, BF16 = jnp.float32, jnp.bfloat16
RADIX = 20
CORES = 2
VMEM_LIMIT = 24 * 1024 * 1024


def split_lat(count):
    side = 1 << (int(math.log2(count)) // 2)
    return count // side, side


def lane_waves(units):
    rows = []
    for c in range(RADIX // 2):
        first, second = (0, RADIX // 2) if c == 0 else (c, RADIX - c)
        rows += [RADIX * u + first for u in range(units)] + [RADIX * u + second for u in range(units)]
    return np.array(rows)


def fourier_table(lon, units):
    inner = lon // RADIX
    waves = lane_waves(units).reshape(RADIX // 4, 4 * units)
    flip = np.ones((RADIX // 2, 2, units))
    flip[1:, 1] = -1.0
    flip = flip.reshape(RADIX // 4, 4 * units)
    phase = waves[:, None, :] * np.arange(inner)[None, :, None] % lon
    cos = np.cos(2 * np.pi * phase / lon) / math.sqrt(lon)
    sin = np.sin(2 * np.pi * phase / lon) / math.sqrt(lon)
    flip = flip[:, None, :]
    top = np.concatenate([cos, -sin], axis=2)
    bottom = np.concatenate([sin * flip, cos * flip], axis=2)
    return np.concatenate([top, bottom], axis=1)


def place(rel, side):
    order = (0, 1, 7, 2, 6, 3, 5, 4).index(rel)
    return side * 5 + order if order < 5 else 10 + side * 3 + order - 5


def dot(a, b, contract=(1, 0)):
    return lax.dot_general(
        a, b, (((contract[0],), (contract[1],)), ((), ())), preferred_element_type=F32
    )


def iota(shape, axis):
    return lax.broadcasted_iota(jnp.int32, shape, axis)


def floor_div(value, divisor):
    return jnp.floor((value.astype(F32) + 0.5) * (1.0 / divisor))


def one_hot(mask):
    return jnp.where(mask, 1.0, 0.0).astype(BF16)


def short_fourier(x, inner):
    part = [x[:, inner * h : inner * (h + 1)] for h in range(RADIX)]
    half = RADIX // 2
    even = [part[h] + part[RADIX - h] for h in range(1, half)]
    odd = [part[h] - part[RADIX - h] for h in range(1, half)]
    real, imag = [None] * (half + 1), [None] * (half + 1)
    for q in range(half // 2 + 1):
        sums = []
        for parity in (0, 1):
            total = None
            for h in range(1, half):
                if h % 2 == parity:
                    factor = math.cos(2 * math.pi * ((q * h) % RADIX) / RADIX)
                    term = even[h - 1] * factor
                    total = term if total is None else total + term
            sums.append(total)
        ends_plus, ends_minus = part[0] + part[half], part[0] - part[half]
        first = sums[0] + (ends_plus if q % 2 == 0 else ends_minus)
        real[q] = first + sums[1]
        if q != half - q:
            other = sums[0] + (ends_plus if (half - q) % 2 == 0 else ends_minus)
            real[half - q] = other - sums[1]
    for q in range(half // 2 + 1):
        sums = []
        for parity in (0, 1):
            total = None
            for h in range(1, half):
                if h % 2 == parity:
                    factor = -math.sin(2 * math.pi * ((q * h) % RADIX) / RADIX)
                    term = odd[h - 1] * factor
                    total = term if total is None else total + term
            sums.append(total)
        imag[q] = sums[0] + sums[1]
        if q != half - q:
            imag[half - q] = sums[1] - sums[0]
    return real, imag


def kernel(
    cfg, hum_hbm, east_hbm, north_hbm, leg_ref, owner_hbm, modes_hbm, values_hbm, table_hbm,
    out_ref,
    hum_ref, east_ref, north_ref, owner_ref, modes_ref, values_ref, table_ref,
    out_buf, x_buf, z_send, z_buf, y_buf, leg_raw, leg_buf, first_buf, last_buf, scale_buf,
    modal_buf,
    load_sem, leg_sem, x_send, x_recv, z_send_sem, z_recv, y_send, y_recv,
):
    nx, nz, ny, slots, levels, trunc, lon, block = (
        cfg[k] for k in ("nx", "nz", "ny", "slots", "levels", "trunc", "lon", "block")
    )
    lev, lat = lax.axis_index("lev"), lax.axis_index("lat")
    x, z = lat // nz, lat % nz
    y, core = lev // CORES, lev % CORES
    inner, units = lon // RADIX, trunc // RADIX
    fields = 3
    piece = 2 * fields * levels
    rows = slots * piece
    width = out_buf.shape[1]
    lats = nx * nz * 2
    total_levels = ny * CORES * levels
    flat = 2 * fields * total_levels
    bundle = 2 * nz
    bundle_z = 2 * nx

    def along_x(i):
        return {"lat": ((x + i) % nx) * nz + z}

    def along_z(i):
        return {"lat": x * nz + (z + i) % nz}

    def along_y(i):
        return {"lev": ((y + i) % ny) * CORES + core}

    partner = {"lev": y * CORES + 1 - core}

    barrier = pltpu.get_barrier_semaphore()
    peers = [along_x(i) for i in range(1, nx)] + [along_z(i) for i in range(1, nz)]
    peers += [along_y(1), along_y(ny - 1), along_y(2), along_y(ny - 2), partner]
    for peer in peers:
        pl.semaphore_signal(barrier, inc=1, device_id=peer, device_id_type=MESH)

    loads = []
    for k, (source, target) in enumerate((
        (owner_hbm, owner_ref), (hum_hbm, hum_ref), (east_hbm, east_ref), (north_hbm, north_ref),
        (table_hbm, table_ref), (modes_hbm, modes_ref), (values_hbm, values_ref),
    )):
        loads.append(pltpu.make_async_copy(source, target, load_sem.at[k]))
        loads[-1].start()
    leg_copy = pltpu.make_async_copy(
        leg_ref.at[:, pl.ds(pl.multiple_of(lev * block, 8), block), :], leg_raw, leg_sem
    )
    leg_copy.start()

    loads[0].wait()
    owner = owner_ref[...].reshape(1, trunc).astype(F32)
    owners = nx * nz
    member = owner == iota((owners, trunc), 0).astype(F32)
    before = one_hot(iota((trunc, trunc), 0) < iota((trunc, trunc), 1))
    count = dot(one_hot(member), before)
    rank = jnp.sum(jnp.where(member, count, 0.0), axis=0, keepdims=True)
    tall_slots = -(-slots // 8) * 8
    mine = (owner == lat.astype(F32)) & (rank == iota((tall_slots, trunc), 0).astype(F32))
    own_waves = jnp.sum(
        jnp.where(mine, iota((tall_slots, trunc), 1).astype(F32), 0.0), axis=1, keepdims=True
    )
    lane = iota((1, trunc), 1)
    clas = floor_div(lane, 2 * units)
    within = lane.astype(F32) - clas * (2 * units)
    second = within >= units
    unit = jnp.where(second, within - units, within)
    residue = jnp.where(second, jnp.where(clas == 0, RADIX // 2, RADIX - clas), clas)
    wave = RADIX * unit + residue
    reorder = one_hot(iota((trunc, trunc), 0).astype(F32) == wave)
    both = jnp.where(iota((16, trunc), 0) == 0, owner, jnp.where(iota((16, trunc), 0) == 1, rank, 0.0))
    both = dot(both.astype(BF16), reorder)
    owner_lane, rank_lane = both[0:1], both[1:2]

    for copy in loads[1:5]:
        copy.wait()
    humidity = hum_ref[...].astype(F32).reshape(2 * levels, lon)
    east = east_ref[...].astype(F32).reshape(2 * levels, lon)
    north = north_ref[...].astype(F32).reshape(2 * levels, lon)
    east = (east * humidity).astype(BF16).astype(F32)
    north = (north * humidity).astype(BF16).astype(F32)
    grid = jnp.concatenate([humidity, east, north], axis=0)
    real, imag = short_fourier(grid, inner)
    joined = [jnp.concatenate([r, i], axis=1) for r, i in zip(real, imag)]
    grid_rows = grid.shape[0]
    reals, imags = [], []
    for p in range(RADIX // 4):
        table = table_ref[p]
        if p == 0:
            left = jnp.concatenate([joined[0], joined[RADIX // 2], joined[1]], axis=0)
            limits = [units, 2 * units]
        else:
            left = jnp.concatenate([joined[2 * p], joined[2 * p + 1]], axis=0)
            limits = [2 * units]
        high = left.astype(BF16)
        low = (left - high.astype(F32)).astype(BF16)
        result = dot(high, table) + dot(low, table) + dot(high, table_ref[RADIX // 4 + p])
        column = iota((grid_rows, 8 * units), 1)
        column = jnp.where(column >= 4 * units, column - 4 * units, column)
        picked = result[len(limits) * grid_rows :]
        for k in reversed(range(len(limits))):
            picked = jnp.where(
                column < limits[k], result[k * grid_rows : (k + 1) * grid_rows], picked
            )
        reals.append(picked[:, : 4 * units])
        imags.append(picked[:, 4 * units :])
    spectrum = jnp.concatenate(
        [jnp.concatenate(reals, axis=1), jnp.concatenate(imags, axis=1)], axis=0
    ).astype(BF16)

    source = iota((piece, 2 * grid_rows), 1)
    target = iota((piece, 2 * grid_rows), 0)
    spread = []
    for t in range(2):
        pick = one_hot(2 * target + t == source)
        spread.append(dot(pick, spectrum))
    halves = []
    for t in range(2):
        pieces = [
            jnp.where(rank_lane == float(s), spread[t], 0.0) for s in range(slots)
        ] + [jnp.zeros((width - rows, trunc), F32)]
        halves.append(jnp.concatenate(pieces, axis=0))
    right = jnp.concatenate(halves, axis=1).astype(BF16)
    row = iota((2 * owners, trunc), 0).astype(F32)
    choose = jnp.concatenate(
        [
            jnp.where(2.0 * owner_lane == row, 1.0, 0.0),
            jnp.where(2.0 * owner_lane + 1.0 == row, 1.0, 0.0),
        ],
        axis=1,
    ).astype(BF16)
    out_buf[...] = dot(choose, right, (1, 1)).astype(BF16)

    pl.semaphore_wait(barrier, len(peers))

    copies = []
    for i in range(1, nx):
        to = (x + i) % nx
        copy = pltpu.make_async_remote_copy(
            src_ref=out_buf.at[pl.ds(pl.multiple_of(to * bundle, bundle), bundle)],
            dst_ref=x_buf.at[pl.ds(pl.multiple_of(x * bundle, bundle), bundle)],
            send_sem=x_send.at[i],
            recv_sem=x_recv.at[i],
            device_id=along_x(i),
            device_id_type=MESH,
        )
        copy.start()
        copies.append(copy)
    x_buf[pl.ds(pl.multiple_of(x * bundle, bundle), bundle), :] = out_buf[
        pl.ds(pl.multiple_of(x * bundle, bundle), bundle), :
    ]

    leg_copy.wait()
    arrive = iota((lats, lats), 1)
    from_z = arrive // bundle_z
    from_x = (arrive % bundle_z) // 2
    reach = one_hot(iota((lats, lats), 0) == (from_x * nz + from_z) * 2 + arrive % 2)
    leg = leg_raw[...].astype(F32).reshape(slots * block, lats).astype(BF16)
    leg = dot(leg, reach)
    degree = iota((block, lats), 0).astype(F32) + (lev * block).astype(F32)
    for s in range(slots):
        live = degree >= own_waves[s : s + 1, :]
        leg_buf[block * s : block * (s + 1), :] = jnp.where(
            live, leg[block * s : block * (s + 1)], 0.0
        )

    swap_to = iota((2 * owners, 2 * owners), 0)
    swap_from = iota((2 * owners, 2 * owners), 1)
    part_z, part_x, part_t = swap_to // bundle_z, (swap_to % bundle_z) // 2, swap_to % 2
    swap = one_hot(swap_from == part_x * bundle + part_z * 2 + part_t)

    for copy in copies:
        copy.wait_recv()
    z_send[...] = dot(swap, x_buf[...]).astype(BF16)
    copies_z = []
    for i in range(1, nz):
        to = (z + i) % nz
        copy = pltpu.make_async_remote_copy(
            src_ref=z_send.at[pl.ds(pl.multiple_of(to * bundle_z, bundle_z), bundle_z)],
            dst_ref=z_buf.at[pl.ds(pl.multiple_of(z * bundle_z, bundle_z), bundle_z)],
            send_sem=z_send_sem.at[i],
            recv_sem=z_recv.at[i],
            device_id=along_z(i),
            device_id_type=MESH,
        )
        copy.start()
        copies_z.append(copy)
    z_buf[pl.ds(pl.multiple_of(z * bundle_z, bundle_z), bundle_z), :] = z_send[
        pl.ds(pl.multiple_of(z * bundle_z, bundle_z), bundle_z), :
    ]

    loads[5].wait()
    loads[6].wait()
    modes = modes_ref[...]
    modes_high = modes.astype(BF16)
    modes_low = (modes - modes_high.astype(F32)).astype(BF16)
    tl = total_levels
    tile = one_hot(iota((tl, flat), 0) == (iota((tl, flat), 1) & (tl - 1)))
    column_part = iota((flat, flat), 1) // tl
    row_id = iota((flat, flat), 0)
    group = floor_div(row_id, piece)
    row_in = row_id.astype(F32) - group * piece
    row_part = floor_div(row_in, levels)
    id64 = iota((flat, tl), 0)
    group64 = floor_div(id64, piece)
    level64 = id64.astype(F32) - group64 * piece
    bases = [None] * (ny * CORES)
    for rel in range(ny):
        for side in range(CORES):
            level_group = ((y + rel) % ny) * CORES + (core if side == 0 else 1 - core)
            bases[place(rel, side)] = jnp.full(
                (piece, tl), (level_group * levels).astype(F32), F32
            )
    level64 = level64 - floor_div(level64, levels) * levels + jnp.concatenate(bases, axis=0)
    gather = one_hot(level64 == iota((flat, tl), 1).astype(F32))
    for k, part in enumerate((modes_high, modes_low)):
        wide = dot(part, tile).astype(BF16)
        first_buf[k] = jnp.where(
            row_part == column_part.astype(F32), dot(gather, wide), 0.0
        ).astype(BF16)
        tall = dot(tile, part, (0, 1)).astype(BF16)
        last_buf[k] = jnp.where(row_id // tl == column_part, dot(tall, tile), 0.0).astype(BF16)
    values = jnp.concatenate([values_ref[...].reshape(1, tl)] * (2 * fields), axis=1)
    number = iota((block, flat), 0).astype(F32) + (lev * block).astype(F32)
    shift = 4.0 * number * (number + 1.0) / (trunc * trunc)
    scale_buf[...] = 1.0 / (1.0 + shift * values)

    for copy in copies_z:
        copy.wait_recv()
    own = z_buf[...].astype(F32).T
    y_buf[place(0, 0)] = own[:rows].astype(BF16)

    pending = []
    half = cfg["half"]

    def message(k, rel, to, to_rel, side, start=0, size=rows):
        return pltpu.make_async_remote_copy(
            src_ref=y_buf.at[place(rel, 0), pl.ds(start, size)],
            dst_ref=y_buf.at[place(to_rel, side), pl.ds(start, size)],
            send_sem=y_send.at[k],
            recv_sem=y_recv.at[k],
            device_id=to,
            device_id_type=MESH,
        )

    def send(k, rel, step, start=0, size=rows):
        copy = message(k, rel, along_y(step % ny), (rel - step) % ny, 0, start, size)
        copy.start()
        pending.append(copy)

    def hand(k, rel):
        copy = message(k, rel, partner, rel, 1)
        copy.start()
        pending.append(copy)

    def arrive_from(k, rel, side, start=0, size=rows):
        pltpu.make_async_remote_copy(
            src_ref=y_buf.at[place(rel, side), pl.ds(start, size)],
            dst_ref=y_buf.at[place(rel, side), pl.ds(start, size)],
            send_sem=y_send.at[k],
            recv_sem=y_recv.at[k],
            device_id=partner,
            device_id_type=MESH,
        ).wait_recv()

    send(0, 0, 2)
    send(1, 0, -2)
    send(2, 0, 1)
    send(3, 0, -1)
    hand(8, 0)
    arrive_from(0, ny - 2, 0)
    send(4, ny - 2, 2, 0, half)
    send(5, ny - 2, 1)
    arrive_from(1, 2, 0)
    send(6, 2, -2, half, rows - half)
    send(7, 2, -1)
    hand(9, ny - 2)
    hand(10, 2)
    arrive_from(2, ny - 1, 0)
    hand(11, ny - 1)
    arrive_from(3, 1, 0)
    hand(12, 1)
    arrive_from(8, 0, 1)
    arrive_from(9, ny - 2, 1)
    arrive_from(10, 2, 1)
    arrive_from(11, ny - 1, 1)
    arrive_from(12, 1, 1)

    def modal_part(first, last):
        pieces = []
        for s in range(slots):
            right = jnp.concatenate(
                [y_buf[g, piece * s : piece * (s + 1), :] for g in range(first, last)], axis=0
            )
            left = leg_buf[block * s : block * (s + 1), :].astype(BF16)
            pieces.append(dot(left, right, (1, 1)))
        projected = jnp.concatenate(pieces, axis=0).astype(BF16)
        span = slice(first * piece, last * piece)
        return dot(projected, first_buf[0, span, :]) + dot(projected, first_buf[1, span, :])

    near, groups = 10, ny * CORES
    modal_buf[...] = modal_part(0, near)
    arrive_from(5, ny - 3, 0)
    hand(13, ny - 3)
    arrive_from(7, 3, 0)
    hand(14, 3)
    arrive_from(4, 4, 0, 0, half)
    arrive_from(6, 4, 0, half, rows - half)
    hand(15, 4)
    modal_buf[...] += modal_part(near, near + 3)
    arrive_from(13, ny - 3, 1)
    arrive_from(14, 3, 1)
    arrive_from(15, 4, 1)
    modal = modal_buf[...] + modal_part(near + 3, groups)
    scale = jnp.concatenate([scale_buf[...]] * slots, axis=0)
    modal = (modal * scale).astype(BF16)
    solved = dot(modal, last_buf[0]) + dot(modal, last_buf[1])
    out_ref[...] = solved.reshape(slots, block, flat)

    for copy in copies + copies_z + pending:
        copy.wait_send()


def build(nx, nz, ny, slots, levels, trunc, lon, half, width):
    block = trunc // (ny * CORES)
    rows = slots * 6 * levels
    total_levels = levels * ny * CORES
    flat = 6 * total_levels
    lats = nx * nz * 2
    inner, units = lon // RADIX, trunc // RADIX
    cfg = dict(
        nx=nx, nz=nz, ny=ny, slots=slots, levels=levels, trunc=trunc, lon=lon, block=block,
        half=half,
    )
    dma = pltpu.SemaphoreType.DMA
    hbm = pl.BlockSpec(memory_space=pltpu.HBM)
    return pl.pallas_call(
        functools.partial(kernel, cfg),
        out_shape=jax.ShapeDtypeStruct((slots, block, flat), F32),
        in_specs=[hbm] * 8,
        out_specs=pl.BlockSpec(memory_space=pltpu.VMEM),
        scratch_shapes=[
            pltpu.VMEM((levels, 2, lon), BF16),
            pltpu.VMEM((levels, 2, lon), BF16),
            pltpu.VMEM((levels, 2, lon), BF16),
            pltpu.VMEM((trunc,), jnp.int32),
            pltpu.VMEM((total_levels, total_levels), F32),
            pltpu.VMEM((total_levels,), F32),
            pltpu.VMEM((RADIX // 2, 2 * inner, 8 * units), BF16),
            pltpu.VMEM((lats, width), BF16),
            pltpu.VMEM((lats, width), BF16),
            pltpu.VMEM((lats, width), BF16),
            pltpu.VMEM((lats, width), BF16),
            pltpu.VMEM((ny * CORES, rows, lats), BF16),
            pltpu.VMEM((slots, block, lats), BF16),
            pltpu.VMEM((slots * block, lats), F32),
            pltpu.VMEM((2, flat, flat), BF16),
            pltpu.VMEM((2, flat, flat), BF16),
            pltpu.VMEM((block, flat), F32),
            pltpu.VMEM((slots * block, flat), F32),
            dma((7,)), dma, dma((nx,)), dma((nx,)), dma((nz,)), dma((nz,)), dma((16,)), dma((16,)),
        ],
        compiler_params=pltpu.CompilerParams(
            collective_id=0, has_side_effects=True, vmem_limit_bytes=VMEM_LIMIT
        ),
    )


def body(humidity, wind_east, wind_north, legendre, owner, vertical_modes, mode_values):
    trunc = owner.shape[0]
    levels, pair, lon = humidity.shape
    owners = lax.axis_size("lat")
    nx, nz = split_lat(owners)
    ny = lax.axis_size("lev") // CORES
    slots = legendre.shape[0]
    rows = slots * 6 * levels
    half = -(-rows // 32) * 16
    width = -(-rows // 128) * 128
    table = fourier_table(lon, trunc // RADIX)
    high = table.astype(BF16)
    table = jnp.asarray(np.concatenate([high, (table - high.astype(np.float64)).astype(BF16)]))
    call = build(nx, nz, ny, slots, levels, trunc, lon, half, width)
    operands = [humidity, wind_east, wind_north, legendre, owner, vertical_modes, mode_values, table]
    return call(*[pltpu.with_memory_space_constraint(v, pltpu.HBM) for v in operands])


def solution(mesh):
    return jax.shard_map(
        body,
        mesh=mesh,
        in_specs=(
            P("lev", "lat", None),
            P("lev", "lat", None),
            P("lev", "lat", None),
            P("lat", None, None),
            P(),
            P(),
            P(),
        ),
        out_specs=P("lat", "lev", None),
        check_vma=False,
    )
```

```python
import functools
import math

import jax
import jax.numpy as jnp
import numpy as np
from jax import lax
from jax.experimental import pallas as pl
from jax.experimental.pallas import tpu as pltpu
from jax.sharding import PartitionSpec as P

MESH = pl.DeviceIdType.MESH
F32, BF16 = jnp.float32, jnp.bfloat16
RADIX = 20
CORES = 2
VMEM_LIMIT = 24 * 1024 * 1024


def split_lat(count):
    side = 1 << (int(math.log2(count)) // 2)
    return count // side, side


def lane_waves(units):
    rows = []
    for c in range(RADIX // 2):
        first, second = (0, RADIX // 2) if c == 0 else (c, RADIX - c)
        rows += [RADIX * u + first for u in range(units)] + [RADIX * u + second for u in range(units)]
    return np.array(rows)


def fourier_table(lon, units):
    inner = lon // RADIX
    waves = lane_waves(units).reshape(RADIX // 4, 4 * units)
    flip = np.ones((RADIX // 2, 2, units))
    flip[1:, 1] = -1.0
    flip = flip.reshape(RADIX // 4, 4 * units)
    phase = waves[:, None, :] * np.arange(inner)[None, :, None] % lon
    cos = np.cos(2 * np.pi * phase / lon) / math.sqrt(lon)
    sin = np.sin(2 * np.pi * phase / lon) / math.sqrt(lon)
    flip = flip[:, None, :]
    top = np.concatenate([cos, -sin], axis=2)
    bottom = np.concatenate([sin * flip, cos * flip], axis=2)
    return np.concatenate([top, bottom], axis=1)


def far_first(size):
    return sorted(range(1, size), key=lambda i: -min(i, size - i))


def place(rel, side):
    order = (0, 1, 7, 2, 6, 3, 5, 4).index(rel)
    return side * 5 + order if order < 5 else 10 + side * 3 + order - 5


def dot(a, b, contract=(1, 0)):
    return lax.dot_general(
        a, b, (((contract[0],), (contract[1],)), ((), ())), preferred_element_type=F32
    )


def iota(shape, axis):
    return lax.broadcasted_iota(jnp.int32, shape, axis)


def floor_div(value, divisor):
    return jnp.floor((value.astype(F32) + 0.5) * (1.0 / divisor))


def one_hot(mask):
    return jnp.where(mask, 1.0, 0.0).astype(BF16)


def short_fourier(x, inner):
    part = [x[:, inner * h : inner * (h + 1)] for h in range(RADIX)]
    half = RADIX // 2
    even = [part[h] + part[RADIX - h] for h in range(1, half)]
    odd = [part[h] - part[RADIX - h] for h in range(1, half)]
    real, imag = [None] * (half + 1), [None] * (half + 1)
    for q in range(half // 2 + 1):
        sums = []
        for parity in (0, 1):
            total = None
            for h in range(1, half):
                if h % 2 == parity:
                    factor = math.cos(2 * math.pi * ((q * h) % RADIX) / RADIX)
                    term = even[h - 1] * factor
                    total = term if total is None else total + term
            sums.append(total)
        ends_plus, ends_minus = part[0] + part[half], part[0] - part[half]
        first = sums[0] + (ends_plus if q % 2 == 0 else ends_minus)
        real[q] = first + sums[1]
        if q != half - q:
            other = sums[0] + (ends_plus if (half - q) % 2 == 0 else ends_minus)
            real[half - q] = other - sums[1]
    for q in range(half // 2 + 1):
        sums = []
        for parity in (0, 1):
            total = None
            for h in range(1, half):
                if h % 2 == parity:
                    factor = -math.sin(2 * math.pi * ((q * h) % RADIX) / RADIX)
                    term = odd[h - 1] * factor
                    total = term if total is None else total + term
            sums.append(total)
        imag[q] = sums[0] + sums[1]
        if q != half - q:
            imag[half - q] = sums[1] - sums[0]
    return real, imag


def kernel(
    cfg, hum_hbm, east_hbm, north_hbm, leg_ref, owner_hbm, modes_hbm, values_hbm, table_hbm,
    out_ref,
    hum_ref, east_ref, north_ref, owner_ref, modes_ref, values_ref, table_ref,
    out_buf, x_buf, z_send, z_buf, y_buf, leg_raw, leg_buf, first_buf, last_buf, scale_buf,
    modal_buf,
    load_sem, leg_sem, x_send, x_recv, z_send_sem, z_recv, y_send, y_recv,
):
    nx, nz, ny, slots, levels, trunc, lon, block = (
        cfg[k] for k in ("nx", "nz", "ny", "slots", "levels", "trunc", "lon", "block")
    )
    lev, lat = lax.axis_index("lev"), lax.axis_index("lat")
    x, z = lat // nz, lat % nz
    y, core = lev // CORES, lev % CORES
    inner, units = lon // RADIX, trunc // RADIX
    fields = 3
    piece = 2 * fields * levels
    rows = slots * piece
    width = out_buf.shape[1]
    wide = width // 2
    half_slots = slots // 2
    lats = nx * nz * 2
    total_levels = ny * CORES * levels
    flat = 2 * fields * total_levels
    bundle = 2 * nz
    bundle_z = 2 * nx

    def along_x(i):
        return {"lat": ((x + i) % nx) * nz + z}

    def along_z(i):
        return {"lat": x * nz + (z + i) % nz}

    def along_y(i):
        return {"lev": ((y + i) % ny) * CORES + core}

    partner = {"lev": y * CORES + 1 - core}

    loads = []
    for k, (source, target) in enumerate((
        (owner_hbm, owner_ref), (hum_hbm, hum_ref), (east_hbm, east_ref), (north_hbm, north_ref),
        (table_hbm, table_ref), (modes_hbm, modes_ref), (values_hbm, values_ref),
    )):
        loads.append(pltpu.make_async_copy(source, target, load_sem.at[k]))
        loads[-1].start()
    barrier = pltpu.get_barrier_semaphore()
    peers = [along_x(i) for i in far_first(nx)] + [along_z(i) for i in far_first(nz)]
    peers += [along_y(2), along_y(ny - 2), along_y(1), along_y(ny - 1), partner]
    for peer in peers:
        pl.semaphore_signal(barrier, inc=1, device_id=peer, device_id_type=MESH)
    leg_copy = pltpu.make_async_copy(
        leg_ref.at[:, pl.ds(pl.multiple_of(lev * block, 8), block), :], leg_raw, leg_sem
    )
    leg_copy.start()

    loads[0].wait()
    owner = owner_ref[...].reshape(1, trunc).astype(F32)
    owners = nx * nz
    member = owner == iota((owners, trunc), 0).astype(F32)
    before = one_hot(iota((trunc, trunc), 0) < iota((trunc, trunc), 1))
    count = dot(one_hot(member), before)
    rank = jnp.sum(jnp.where(member, count, 0.0), axis=0, keepdims=True)
    tall_slots = -(-slots // 8) * 8
    mine = (owner == lat.astype(F32)) & (rank == iota((tall_slots, trunc), 0).astype(F32))
    own_waves = jnp.sum(
        jnp.where(mine, iota((tall_slots, trunc), 1).astype(F32), 0.0), axis=1, keepdims=True
    )
    lane = iota((1, trunc), 1)
    clas = floor_div(lane, 2 * units)
    within = lane.astype(F32) - clas * (2 * units)
    second = within >= units
    unit = jnp.where(second, within - units, within)
    residue = jnp.where(second, jnp.where(clas == 0, RADIX // 2, RADIX - clas), clas)
    wave = RADIX * unit + residue
    reorder = one_hot(iota((trunc, trunc), 0).astype(F32) == wave)
    both = jnp.where(iota((16, trunc), 0) == 0, owner, jnp.where(iota((16, trunc), 0) == 1, rank, 0.0))
    both = dot(both.astype(BF16), reorder)
    owner_lane, rank_lane = both[0:1], both[1:2]

    for copy in loads[1:5]:
        copy.wait()
    humidity = hum_ref[...].astype(F32).reshape(2 * levels, lon)
    east = east_ref[...].astype(F32).reshape(2 * levels, lon)
    north = north_ref[...].astype(F32).reshape(2 * levels, lon)
    east = (east * humidity).astype(BF16).astype(F32)
    north = (north * humidity).astype(BF16).astype(F32)
    grid = jnp.concatenate([humidity, east, north], axis=0)
    real, imag = short_fourier(grid, inner)
    joined = [jnp.concatenate([r, i], axis=1) for r, i in zip(real, imag)]
    grid_rows = grid.shape[0]
    reals, imags = [], []
    for p in range(RADIX // 4):
        table = table_ref[p]
        if p == 0:
            left = jnp.concatenate([joined[0], joined[RADIX // 2], joined[1]], axis=0)
            limits = [units, 2 * units]
        else:
            left = jnp.concatenate([joined[2 * p], joined[2 * p + 1]], axis=0)
            limits = [2 * units]
        high = left.astype(BF16)
        low = (left - high.astype(F32)).astype(BF16)
        result = dot(high, table) + dot(low, table) + dot(high, table_ref[RADIX // 4 + p])
        column = iota((grid_rows, 8 * units), 1)
        column = jnp.where(column >= 4 * units, column - 4 * units, column)
        picked = result[len(limits) * grid_rows :]
        for k in reversed(range(len(limits))):
            picked = jnp.where(
                column < limits[k], result[k * grid_rows : (k + 1) * grid_rows], picked
            )
        reals.append(picked[:, : 4 * units])
        imags.append(picked[:, 4 * units :])
    spectrum = jnp.concatenate(
        [jnp.concatenate(reals, axis=1), jnp.concatenate(imags, axis=1)], axis=0
    ).astype(BF16)

    source = iota((piece, 2 * grid_rows), 1)
    target = iota((piece, 2 * grid_rows), 0)
    spread = []
    for t in range(2):
        pick = one_hot(2 * target + t == source)
        spread.append(dot(pick, spectrum))
    halves = []
    for t in range(2):
        pieces = []
        for s in range(slots):
            pieces.append(jnp.where(rank_lane == float(s), spread[t], 0.0))
            if (s + 1) % half_slots == 0 and wide > half_slots * piece:
                pieces.append(jnp.zeros((wide - half_slots * piece, trunc), F32))
        halves.append(jnp.concatenate(pieces, axis=0))
    right = jnp.concatenate(halves, axis=1).astype(BF16)
    row = iota((2 * owners, trunc), 0).astype(F32)
    choose = jnp.concatenate(
        [
            jnp.where(2.0 * owner_lane == row, 1.0, 0.0),
            jnp.where(2.0 * owner_lane + 1.0 == row, 1.0, 0.0),
        ],
        axis=1,
    ).astype(BF16)
    out_buf[...] = dot(choose, right, (1, 1)).astype(BF16)

    pl.semaphore_wait(barrier, len(peers))

    copies = []
    for i in far_first(nx):
        to = (x + i) % nx
        copy = pltpu.make_async_remote_copy(
            src_ref=out_buf.at[pl.ds(pl.multiple_of(to * bundle, bundle), bundle)],
            dst_ref=x_buf.at[pl.ds(pl.multiple_of(x * bundle, bundle), bundle)],
            send_sem=x_send.at[i],
            recv_sem=x_recv.at[i],
            device_id=along_x(i),
            device_id_type=MESH,
        )
        copy.start()
        copies.append(copy)
    x_buf[pl.ds(pl.multiple_of(x * bundle, bundle), bundle), :] = out_buf[
        pl.ds(pl.multiple_of(x * bundle, bundle), bundle), :
    ]

    leg_copy.wait()
    lane = iota((lats, lats), 1)
    arrive = lane % owners
    leg = leg_raw[...].astype(F32).reshape(slots * block, lats).astype(BF16)
    degree = iota((block, lats), 0).astype(F32) + (lev * block).astype(F32)
    for h in range(2):
        from_z = arrive // bundle_z + h * (nz // 2)
        from_x = (arrive % bundle_z) // 2
        reach = iota((lats, lats), 0) == (from_x * nz + from_z) * 2 + arrive % 2
        for part in range(2):
            span = half_slots * block
            turned = dot(
                leg[part * span : (part + 1) * span], one_hot(reach & (lane // owners == part))
            )
            for k in range(half_slots):
                s = part * half_slots + k
                live = degree >= own_waves[s : s + 1, :]
                leg_buf[h, block * s : block * (s + 1), :] = jnp.where(
                    live, turned[block * k : block * (k + 1)], 0.0
                )

    swap_to = iota((2 * owners, 2 * owners), 0)
    swap_from = iota((2 * owners, 2 * owners), 1)
    part_z, part_x, part_t = swap_to // bundle_z, (swap_to % bundle_z) // 2, swap_to % 2
    swap = one_hot(swap_from == part_x * bundle + part_z * 2 + part_t)

    loads[5].wait()
    loads[6].wait()
    modes = modes_ref[...]
    modes_high = modes.astype(BF16)
    modes_low = (modes - modes_high.astype(F32)).astype(BF16)
    tl = total_levels
    tile = one_hot(iota((tl, flat), 0) == (iota((tl, flat), 1) & (tl - 1)))
    column_part = iota((flat, flat), 1) // tl
    row_id = iota((flat, flat), 0)
    group = floor_div(row_id, piece)
    row_in = row_id.astype(F32) - group * piece
    row_part = floor_div(row_in, levels)
    id64 = iota((flat, tl), 0)
    group64 = floor_div(id64, piece)
    level64 = id64.astype(F32) - group64 * piece
    bases = [None] * (ny * CORES)
    for rel in range(ny):
        for side in range(CORES):
            level_group = ((y + rel) % ny) * CORES + (core if side == 0 else 1 - core)
            bases[place(rel, side)] = jnp.full(
                (piece, tl), (level_group * levels).astype(F32), F32
            )
    level64 = level64 - floor_div(level64, levels) * levels + jnp.concatenate(bases, axis=0)
    gather = one_hot(level64 == iota((flat, tl), 1).astype(F32))
    for k, part in enumerate((modes_high, modes_low)):
        stretched = dot(part, tile).astype(BF16)
        first_buf[k] = jnp.where(
            row_part == column_part.astype(F32), dot(gather, stretched), 0.0
        ).astype(BF16)
        tall = dot(tile, part, (0, 1)).astype(BF16)
        last_buf[k] = jnp.where(row_id // tl == column_part, dot(tall, tile), 0.0).astype(BF16)
    values = jnp.concatenate([values_ref[...].reshape(1, tl)] * (2 * fields), axis=1)
    number = iota((block, flat), 0).astype(F32) + (lev * block).astype(F32)
    shift = 4.0 * number * (number + 1.0) / (trunc * trunc)
    scale_buf[...] = 1.0 / (1.0 + shift * values)

    for copy in copies:
        copy.wait_recv()
    z_send[...] = dot(swap, x_buf[...]).astype(BF16)
    copies_z = []
    for i in far_first(nz):
        to = (z + i) % nz
        copy = pltpu.make_async_remote_copy(
            src_ref=z_send.at[pl.ds(pl.multiple_of(to * bundle_z, bundle_z), bundle_z)],
            dst_ref=z_buf.at[pl.ds(pl.multiple_of(z * bundle_z, bundle_z), bundle_z)],
            send_sem=z_send_sem.at[i],
            recv_sem=z_recv.at[z],
            device_id=along_z(i),
            device_id_type=MESH,
        )
        copy.start()
        copies_z.append(copy)
    z_buf[pl.ds(pl.multiple_of(z * bundle_z, bundle_z), bundle_z), :] = z_send[
        pl.ds(pl.multiple_of(z * bundle_z, bundle_z), bundle_z), :
    ]

    pending = []
    cut = cfg["cut"]

    def fill(h):
        for source in range(h * nz // 2, (h + 1) * nz // 2):
            @pl.when(source != z)
            def _():
                view = z_buf.at[pl.ds(source * bundle_z, bundle_z)]
                pltpu.make_async_remote_copy(
                    src_ref=view, dst_ref=view, send_sem=z_send_sem.at[0],
                    recv_sem=z_recv.at[source], device_id=partner, device_id_type=MESH,
                ).wait_recv()

        own = z_buf[owners * h : owners * (h + 1), :].astype(F32)
        own = jnp.concatenate([own[:, :wide], own[:, wide:]], axis=0)
        y_buf[h, place(0, 0)] = own.T.astype(BF16)

    def message(h, k, rel, to, to_rel, side, start=0, size=wide):
        return pltpu.make_async_remote_copy(
            src_ref=y_buf.at[h, place(rel, 0), pl.ds(start, size)],
            dst_ref=y_buf.at[h, place(to_rel, side), pl.ds(start, size)],
            send_sem=y_send.at[h, k],
            recv_sem=y_recv.at[h, k],
            device_id=to,
            device_id_type=MESH,
        )

    def send(h, k, rel, step, start=0, size=wide):
        copy = message(h, k, rel, along_y(step % ny), (rel - step) % ny, 0, start, size)
        copy.start()
        pending.append(copy)

    def hand(h, k, rel):
        copy = message(h, k, rel, partner, rel, 1)
        copy.start()
        pending.append(copy)

    def arrival(h, k, rel, side, start=0, size=wide):
        view = y_buf.at[h, place(rel, side), pl.ds(start, size)]
        pltpu.make_async_remote_copy(
            src_ref=view, dst_ref=view, send_sem=y_send.at[h, k], recv_sem=y_recv.at[h, k],
            device_id=partner, device_id_type=MESH,
        ).wait_recv()

    def first_step(h):
        send(h, 0, 0, 2)
        send(h, 1, 0, -2)
        send(h, 2, 0, 1)
        send(h, 3, 0, -1)
        hand(h, 8, 0)

    def second_step(h):
        arrival(h, 0, ny - 2, 0)
        send(h, 4, ny - 2, 2, 0, cut)
        send(h, 5, ny - 2, 1)
        arrival(h, 1, 2, 0)
        send(h, 6, 2, -2, cut, wide - cut)
        send(h, 7, 2, -1)
        hand(h, 9, ny - 2)
        hand(h, 10, 2)
        arrival(h, 2, ny - 1, 0)
        hand(h, 11, ny - 1)
        arrival(h, 3, 1, 0)
        hand(h, 12, 1)

    def last_step(h):
        arrival(h, 5, ny - 3, 0)
        hand(h, 13, ny - 3)
        arrival(h, 7, 3, 0)
        hand(h, 14, 3)
        arrival(h, 4, 4, 0, 0, cut)
        arrival(h, 6, 4, 0, cut, wide - cut)
        hand(h, 15, 4)

    def near_handed(h):
        for k, rel in ((8, 0), (9, ny - 2), (10, 2), (11, ny - 1), (12, 1)):
            arrival(h, k, rel, 1)

    def far_handed(h):
        for k, rel in ((13, ny - 3), (14, 3), (15, 4)):
            arrival(h, k, rel, 1)

    def modal_part(h, first, last):
        pieces = []
        for s in range(slots):
            rows_of = slice(piece * (s % half_slots), piece * (s % half_slots + 1))
            right = jnp.concatenate([y_buf[h, g, rows_of, :] for g in range(first, last)], axis=0)
            left = leg_buf[h, block * s : block * (s + 1), :].astype(BF16)
            pieces.append(dot(left, right, (1, 1)))
        projected = jnp.concatenate(pieces, axis=0).astype(BF16)
        span = slice(first * piece, last * piece)
        return dot(projected, first_buf[0, span, :]) + dot(projected, first_buf[1, span, :])

    near, groups = 10, ny * CORES
    fill(0)
    first_step(0)
    second_step(0)
    fill(1)
    first_step(1)
    last_step(0)
    second_step(1)
    near_handed(0)
    far_handed(0)
    modal_buf[...] = modal_part(0, 0, groups)
    near_handed(1)
    modal_buf[...] += modal_part(1, 0, near)
    last_step(1)
    modal_buf[...] += modal_part(1, near, near + 3)
    far_handed(1)
    modal = modal_buf[...] + modal_part(1, near + 3, groups)
    scale = jnp.concatenate([scale_buf[...]] * slots, axis=0)
    modal = (modal * scale).astype(BF16)
    solved = dot(modal, last_buf[0]) + dot(modal, last_buf[1])
    out_ref[...] = solved.reshape(slots, block, flat)

    for copy in copies + copies_z + pending:
        copy.wait_send()


def build(nx, nz, ny, slots, levels, trunc, lon, cut, width):
    block = trunc // (ny * CORES)
    total_levels = levels * ny * CORES
    flat = 6 * total_levels
    lats = nx * nz * 2
    inner, units = lon // RADIX, trunc // RADIX
    cfg = dict(
        nx=nx, nz=nz, ny=ny, slots=slots, levels=levels, trunc=trunc, lon=lon, block=block,
        cut=cut,
    )
    dma = pltpu.SemaphoreType.DMA
    hbm = pl.BlockSpec(memory_space=pltpu.HBM)
    return pl.pallas_call(
        functools.partial(kernel, cfg),
        out_shape=jax.ShapeDtypeStruct((slots, block, flat), F32),
        in_specs=[hbm] * 8,
        out_specs=pl.BlockSpec(memory_space=pltpu.VMEM),
        scratch_shapes=[
            pltpu.VMEM((levels, 2, lon), BF16),
            pltpu.VMEM((levels, 2, lon), BF16),
            pltpu.VMEM((levels, 2, lon), BF16),
            pltpu.VMEM((trunc,), jnp.int32),
            pltpu.VMEM((total_levels, total_levels), F32),
            pltpu.VMEM((total_levels,), F32),
            pltpu.VMEM((RADIX // 2, 2 * inner, 8 * units), BF16),
            pltpu.VMEM((lats, width), BF16),
            pltpu.VMEM((lats, width), BF16),
            pltpu.VMEM((lats, width), BF16),
            pltpu.VMEM((lats, width), BF16),
            pltpu.VMEM((2, ny * CORES, width // 2, lats), BF16),
            pltpu.VMEM((slots, block, lats), BF16),
            pltpu.VMEM((2, slots * block, lats), F32),
            pltpu.VMEM((2, flat, flat), BF16),
            pltpu.VMEM((2, flat, flat), BF16),
            pltpu.VMEM((block, flat), F32),
            pltpu.VMEM((slots * block, flat), F32),
            dma((7,)), dma, dma((nx,)), dma((nx,)), dma((nz,)), dma((nz,)), dma((2, 16)), dma((2, 16)),
        ],
        compiler_params=pltpu.CompilerParams(
            collective_id=0, has_side_effects=True, vmem_limit_bytes=VMEM_LIMIT
        ),
    )


def body(humidity, wind_east, wind_north, legendre, owner, vertical_modes, mode_values):
    trunc = owner.shape[0]
    levels, pair, lon = humidity.shape
    owners = lax.axis_size("lat")
    nx, nz = split_lat(owners)
    ny = lax.axis_size("lev") // CORES
    slots = legendre.shape[0]
    rows = slots * 6 * levels
    width = 2 * (-(-rows // 256) * 128)
    cut = width // 4
    table = fourier_table(lon, trunc // RADIX)
    high = table.astype(BF16)
    table = jnp.asarray(np.concatenate([high, (table - high.astype(np.float64)).astype(BF16)]))
    call = build(nx, nz, ny, slots, levels, trunc, lon, cut, width)
    operands = [humidity, wind_east, wind_north, legendre, owner, vertical_modes, mode_values, table]
    return call(*[pltpu.with_memory_space_constraint(v, pltpu.HBM) for v in operands])


def solution(mesh):
    return jax.shard_map(
        body,
        mesh=mesh,
        in_specs=(
            P("lev", "lat", None),
            P("lev", "lat", None),
            P("lev", "lat", None),
            P("lat", None, None),
            P(),
            P(),
            P(),
        ),
        out_specs=P("lat", "lev", None),
        check_vma=False,
    )
```

```python
import functools
import math

import jax
import jax.numpy as jnp
import numpy as np
from jax import lax
from jax.experimental import pallas as pl
from jax.experimental.pallas import tpu as pltpu
from jax.sharding import PartitionSpec as P

MESH = pl.DeviceIdType.MESH
F32, BF16 = jnp.float32, jnp.bfloat16
RADIX = 20
CORES = 2
VMEM_LIMIT = 24 * 1024 * 1024


def split_lat(count):
    side = 1 << (int(math.log2(count)) // 2)
    return count // side, side


def lane_waves(units):
    rows = []
    for c in range(RADIX // 2):
        first, second = (0, RADIX // 2) if c == 0 else (c, RADIX - c)
        rows += [RADIX * u + first for u in range(units)] + [RADIX * u + second for u in range(units)]
    return np.array(rows)


def fourier_table(lon, units):
    inner = lon // RADIX
    waves = lane_waves(units).reshape(RADIX // 4, 4 * units)
    flip = np.ones((RADIX // 2, 2, units))
    flip[1:, 1] = -1.0
    flip = flip.reshape(RADIX // 4, 4 * units)
    phase = waves[:, None, :] * np.arange(inner)[None, :, None] % lon
    cos = np.cos(2 * np.pi * phase / lon) / math.sqrt(lon)
    sin = np.sin(2 * np.pi * phase / lon) / math.sqrt(lon)
    flip = flip[:, None, :]
    top = np.concatenate([cos, -sin], axis=2)
    bottom = np.concatenate([sin * flip, cos * flip], axis=2)
    return np.concatenate([top, bottom], axis=1)


def far_first(size):
    return sorted(range(1, size), key=lambda i: -min(i, size - i))


def place(rel, side):
    order = (0, 1, 7, 2, 6, 3, 5, 4).index(rel)
    return side * 5 + order if order < 5 else 10 + side * 3 + order - 5


def dot(a, b, contract=(1, 0)):
    return lax.dot_general(
        a, b, (((contract[0],), (contract[1],)), ((), ())), preferred_element_type=F32
    )


def iota(shape, axis):
    return lax.broadcasted_iota(jnp.int32, shape, axis)


def floor_div(value, divisor):
    return jnp.floor((value.astype(F32) + 0.5) * (1.0 / divisor))


def one_hot(mask):
    return jnp.where(mask, 1.0, 0.0).astype(BF16)


def short_fourier(x, inner):
    part = [x[:, inner * h : inner * (h + 1)] for h in range(RADIX)]
    half = RADIX // 2
    even = [part[h] + part[RADIX - h] for h in range(1, half)]
    odd = [part[h] - part[RADIX - h] for h in range(1, half)]
    real, imag = [None] * (half + 1), [None] * (half + 1)
    for q in range(half // 2 + 1):
        sums = []
        for parity in (0, 1):
            total = None
            for h in range(1, half):
                if h % 2 == parity:
                    factor = math.cos(2 * math.pi * ((q * h) % RADIX) / RADIX)
                    term = even[h - 1] * factor
                    total = term if total is None else total + term
            sums.append(total)
        ends_plus, ends_minus = part[0] + part[half], part[0] - part[half]
        first = sums[0] + (ends_plus if q % 2 == 0 else ends_minus)
        real[q] = first + sums[1]
        if q != half - q:
            other = sums[0] + (ends_plus if (half - q) % 2 == 0 else ends_minus)
            real[half - q] = other - sums[1]
    for q in range(half // 2 + 1):
        sums = []
        for parity in (0, 1):
            total = None
            for h in range(1, half):
                if h % 2 == parity:
                    factor = -math.sin(2 * math.pi * ((q * h) % RADIX) / RADIX)
                    term = odd[h - 1] * factor
                    total = term if total is None else total + term
            sums.append(total)
        imag[q] = sums[0] + sums[1]
        if q != half - q:
            imag[half - q] = sums[1] - sums[0]
    return real, imag


def kernel(
    cfg, hum_hbm, east_hbm, north_hbm, leg_ref, owner_hbm, modes_hbm, values_hbm, table_hbm,
    out_ref,
    hum_ref, east_ref, north_ref, owner_ref, modes_ref, values_ref, table_ref,
    out_buf, x_buf, z_send, z_buf, y_buf, leg_raw, leg_buf, first_buf, last_buf, scale_buf,
    modal_buf,
    load_sem, leg_sem, x_send, x_recv, z_send_sem, z_recv, y_send, y_recv,
):
    nx, nz, ny, slots, levels, trunc, lon, block = (
        cfg[k] for k in ("nx", "nz", "ny", "slots", "levels", "trunc", "lon", "block")
    )
    lev, lat = lax.axis_index("lev"), lax.axis_index("lat")
    x, z = lat // nz, lat % nz
    y, core = lev // CORES, lev % CORES
    inner, units = lon // RADIX, trunc // RADIX
    fields = 3
    piece = 2 * fields * levels
    rows = slots * piece
    width = out_buf.shape[1]
    lats = nx * nz * 2
    total_levels = ny * CORES * levels
    flat = 2 * fields * total_levels
    bundle = 2 * nz
    bundle_z = 2 * nx

    def along_x(i):
        return {"lat": ((x + i) % nx) * nz + z}

    def along_z(i):
        return {"lat": x * nz + (z + i) % nz}

    def along_y(i):
        return {"lev": ((y + i) % ny) * CORES + core}

    partner = {"lev": y * CORES + 1 - core}

    loads = []
    for k, (source, target) in enumerate((
        (owner_hbm, owner_ref), (hum_hbm, hum_ref), (east_hbm, east_ref), (north_hbm, north_ref),
        (table_hbm, table_ref), (modes_hbm, modes_ref), (values_hbm, values_ref),
    )):
        loads.append(pltpu.make_async_copy(source, target, load_sem.at[k]))
        loads[-1].start()
    barrier = pltpu.get_barrier_semaphore()
    peers = [along_x(i) for i in far_first(nx)] + [along_z(i) for i in far_first(nz)]
    peers += [along_y(2), along_y(ny - 2), along_y(1), along_y(ny - 1), partner]
    for peer in peers:
        pl.semaphore_signal(barrier, inc=1, device_id=peer, device_id_type=MESH)
    leg_copy = pltpu.make_async_copy(
        leg_ref.at[:, pl.ds(pl.multiple_of(lev * block, 8), block), :], leg_raw, leg_sem
    )
    leg_copy.start()

    loads[0].wait()
    owner = owner_ref[...].reshape(1, trunc).astype(F32)
    owners = nx * nz
    member = owner == iota((owners, trunc), 0).astype(F32)
    before = one_hot(iota((trunc, trunc), 0) < iota((trunc, trunc), 1))
    count = dot(one_hot(member), before)
    rank = jnp.sum(jnp.where(member, count, 0.0), axis=0, keepdims=True)
    tall_slots = -(-slots // 8) * 8
    mine = (owner == lat.astype(F32)) & (rank == iota((tall_slots, trunc), 0).astype(F32))
    own_waves = jnp.sum(
        jnp.where(mine, iota((tall_slots, trunc), 1).astype(F32), 0.0), axis=1, keepdims=True
    )
    lane = iota((1, trunc), 1)
    clas = floor_div(lane, 2 * units)
    within = lane.astype(F32) - clas * (2 * units)
    second = within >= units
    unit = jnp.where(second, within - units, within)
    residue = jnp.where(second, jnp.where(clas == 0, RADIX // 2, RADIX - clas), clas)
    wave = RADIX * unit + residue
    reorder = one_hot(iota((trunc, trunc), 0).astype(F32) == wave)
    both = jnp.where(iota((16, trunc), 0) == 0, owner, jnp.where(iota((16, trunc), 0) == 1, rank, 0.0))
    both = dot(both.astype(BF16), reorder)
    owner_lane, rank_lane = both[0:1], both[1:2]

    for copy in loads[1:5]:
        copy.wait()
    humidity = hum_ref[...].astype(F32).reshape(2 * levels, lon)
    east = east_ref[...].astype(F32).reshape(2 * levels, lon)
    north = north_ref[...].astype(F32).reshape(2 * levels, lon)
    east = (east * humidity).astype(BF16).astype(F32)
    north = (north * humidity).astype(BF16).astype(F32)
    grid = jnp.concatenate([humidity, east, north], axis=0)
    real, imag = short_fourier(grid, inner)
    joined = [jnp.concatenate([r, i], axis=1) for r, i in zip(real, imag)]
    grid_rows = grid.shape[0]
    reals, imags = [], []
    for p in range(RADIX // 4):
        table = table_ref[p]
        if p == 0:
            left = jnp.concatenate([joined[0], joined[RADIX // 2], joined[1]], axis=0)
            limits = [units, 2 * units]
        else:
            left = jnp.concatenate([joined[2 * p], joined[2 * p + 1]], axis=0)
            limits = [2 * units]
        high = left.astype(BF16)
        low = (left - high.astype(F32)).astype(BF16)
        result = dot(high, table) + dot(low, table) + dot(high, table_ref[RADIX // 4 + p])
        column = iota((grid_rows, 8 * units), 1)
        column = jnp.where(column >= 4 * units, column - 4 * units, column)
        picked = result[len(limits) * grid_rows :]
        for k in reversed(range(len(limits))):
            picked = jnp.where(
                column < limits[k], result[k * grid_rows : (k + 1) * grid_rows], picked
            )
        reals.append(picked[:, : 4 * units])
        imags.append(picked[:, 4 * units :])
    spectrum = jnp.concatenate(
        [jnp.concatenate(reals, axis=1), jnp.concatenate(imags, axis=1)], axis=0
    ).astype(BF16)

    source = iota((piece, 2 * grid_rows), 1)
    target = iota((piece, 2 * grid_rows), 0)
    spread = []
    for t in range(2):
        pick = one_hot(2 * target + t == source)
        spread.append(dot(pick, spectrum))
    halves = []
    for t in range(2):
        pieces = [
            jnp.where(rank_lane == float(s), spread[t], 0.0) for s in range(slots)
        ] + [jnp.zeros((width - rows, trunc), F32)]
        halves.append(jnp.concatenate(pieces, axis=0))
    right = jnp.concatenate(halves, axis=1).astype(BF16)
    row = iota((2 * owners, trunc), 0).astype(F32)
    choose = jnp.concatenate(
        [
            jnp.where(2.0 * owner_lane == row, 1.0, 0.0),
            jnp.where(2.0 * owner_lane + 1.0 == row, 1.0, 0.0),
        ],
        axis=1,
    ).astype(BF16)
    out_buf[...] = dot(choose, right, (1, 1)).astype(BF16)

    pl.semaphore_wait(barrier, len(peers))

    copies = []
    for i in far_first(nx):
        to = (x + i) % nx
        copy = pltpu.make_async_remote_copy(
            src_ref=out_buf.at[pl.ds(pl.multiple_of(to * bundle, bundle), bundle)],
            dst_ref=x_buf.at[pl.ds(pl.multiple_of(x * bundle, bundle), bundle)],
            send_sem=x_send.at[i],
            recv_sem=x_recv.at[i],
            device_id=along_x(i),
            device_id_type=MESH,
        )
        copy.start()
        copies.append(copy)
    x_buf[pl.ds(pl.multiple_of(x * bundle, bundle), bundle), :] = out_buf[
        pl.ds(pl.multiple_of(x * bundle, bundle), bundle), :
    ]

    leg_copy.wait()
    arrive = iota((lats, lats), 1)
    from_z = arrive // bundle_z
    from_x = (arrive % bundle_z) // 2
    reach = one_hot(iota((lats, lats), 0) == (from_x * nz + from_z) * 2 + arrive % 2)
    leg = leg_raw[...].astype(F32).reshape(slots * block, lats).astype(BF16)
    leg = dot(leg, reach)
    degree = iota((block, lats), 0).astype(F32) + (lev * block).astype(F32)
    for s in range(slots):
        live = degree >= own_waves[s : s + 1, :]
        leg_buf[block * s : block * (s + 1), :] = jnp.where(
            live, leg[block * s : block * (s + 1)], 0.0
        )

    swap_to = iota((2 * owners, 2 * owners), 0)
    swap_from = iota((2 * owners, 2 * owners), 1)
    part_z, part_x, part_t = swap_to // bundle_z, (swap_to % bundle_z) // 2, swap_to % 2
    swap = one_hot(swap_from == part_x * bundle + part_z * 2 + part_t)

    loads[5].wait()
    loads[6].wait()
    modes = modes_ref[...]
    modes_high = modes.astype(BF16)
    modes_low = (modes - modes_high.astype(F32)).astype(BF16)
    tl = total_levels
    tile = one_hot(iota((tl, flat), 0) == (iota((tl, flat), 1) & (tl - 1)))
    column_part = iota((flat, flat), 1) // tl
    row_id = iota((flat, flat), 0)
    group = floor_div(row_id, piece)
    row_in = row_id.astype(F32) - group * piece
    row_part = floor_div(row_in, levels)
    id64 = iota((flat, tl), 0)
    group64 = floor_div(id64, piece)
    level64 = id64.astype(F32) - group64 * piece
    bases = [None] * (ny * CORES)
    for rel in range(ny):
        for side in range(CORES):
            level_group = ((y + rel) % ny) * CORES + (core if side == 0 else 1 - core)
            bases[place(rel, side)] = jnp.full(
                (piece, tl), (level_group * levels).astype(F32), F32
            )
    level64 = level64 - floor_div(level64, levels) * levels + jnp.concatenate(bases, axis=0)
    gather = one_hot(level64 == iota((flat, tl), 1).astype(F32))
    for k, part in enumerate((modes_high, modes_low)):
        wide = dot(part, tile).astype(BF16)
        first_buf[k] = jnp.where(
            row_part == column_part.astype(F32), dot(gather, wide), 0.0
        ).astype(BF16)
        tall = dot(tile, part, (0, 1)).astype(BF16)
        last_buf[k] = jnp.where(row_id // tl == column_part, dot(tall, tile), 0.0).astype(BF16)
    values = jnp.concatenate([values_ref[...].reshape(1, tl)] * (2 * fields), axis=1)
    number = iota((block, flat), 0).astype(F32) + (lev * block).astype(F32)
    shift = 4.0 * number * (number + 1.0) / (trunc * trunc)
    scale_buf[...] = 1.0 / (1.0 + shift * values)

    for copy in copies:
        copy.wait_recv()
    z_send[...] = dot(swap, x_buf[...]).astype(BF16)
    copies_z = []
    for i in far_first(nz):
        to = (z + i) % nz
        copy = pltpu.make_async_remote_copy(
            src_ref=z_send.at[pl.ds(pl.multiple_of(to * bundle_z, bundle_z), bundle_z)],
            dst_ref=z_buf.at[pl.ds(pl.multiple_of(z * bundle_z, bundle_z), bundle_z)],
            send_sem=z_send_sem.at[i],
            recv_sem=z_recv.at[i],
            device_id=along_z(i),
            device_id_type=MESH,
        )
        copy.start()
        copies_z.append(copy)
    z_buf[pl.ds(pl.multiple_of(z * bundle_z, bundle_z), bundle_z), :] = z_send[
        pl.ds(pl.multiple_of(z * bundle_z, bundle_z), bundle_z), :
    ]

    for copy in copies_z:
        copy.wait_recv()
    own = z_buf[...].astype(F32).T
    y_buf[place(0, 0)] = own[:rows].astype(BF16)

    pending = []
    half = cfg["half"]

    def message(k, rel, to, to_rel, side, start=0, size=rows):
        return pltpu.make_async_remote_copy(
            src_ref=y_buf.at[place(rel, 0), pl.ds(start, size)],
            dst_ref=y_buf.at[place(to_rel, side), pl.ds(start, size)],
            send_sem=y_send.at[k],
            recv_sem=y_recv.at[k],
            device_id=to,
            device_id_type=MESH,
        )

    def send(k, rel, step, start=0, size=rows):
        copy = message(k, rel, along_y(step % ny), (rel - step) % ny, 0, start, size)
        copy.start()
        return copy

    def relay(*args):
        pending.append(send(*args))

    def hand(k, rel, start=0, size=rows):
        copy = message(k, rel, partner, rel, 1, start, size)
        copy.start()
        pending.append(copy)

    def arrive_from(k, rel, side, start=0, size=rows):
        view = y_buf.at[place(rel, side), pl.ds(start, size)]
        pltpu.make_async_remote_copy(
            src_ref=view, dst_ref=view, send_sem=y_send.at[k], recv_sem=y_recv.at[k],
            device_id=partner, device_id_type=MESH,
        ).wait_recv()

    lower, upper = (0, half), (half, rows - half)
    below, above = ny - 2, 2
    for up, down in ((lower, upper), (upper, lower)):
        k = 0 if up == lower else 2
        first = send(k, 0, 2, *up), send(k + 1, 0, -2, *down)
        for copy in first:
            copy.wait_send()
    relay(4, 0, 1)
    relay(5, 0, -1)
    hand(12, 0)
    arrive_from(0, below, 0, *lower)
    relay(6, below, 2, *lower)
    relay(8, below, 1, *lower)
    arrive_from(1, above, 0, *upper)
    relay(7, above, -2, *upper)
    relay(9, above, -1, *upper)
    arrive_from(2, below, 0, *upper)
    relay(10, below, 1, *upper)
    arrive_from(3, above, 0, *lower)
    relay(11, above, -1, *lower)
    hand(13, below)
    hand(14, above)
    arrive_from(4, ny - 1, 0)
    hand(15, ny - 1)
    arrive_from(5, 1, 0)
    hand(16, 1)
    arrive_from(12, 0, 1)
    arrive_from(13, below, 1)
    arrive_from(14, above, 1)
    arrive_from(15, ny - 1, 1)
    arrive_from(16, 1, 1)

    def modal_part(first, last):
        pieces = []
        for s in range(slots):
            right = jnp.concatenate(
                [y_buf[g, piece * s : piece * (s + 1), :] for g in range(first, last)], axis=0
            )
            left = leg_buf[block * s : block * (s + 1), :].astype(BF16)
            pieces.append(dot(left, right, (1, 1)))
        projected = jnp.concatenate(pieces, axis=0).astype(BF16)
        span = slice(first * piece, last * piece)
        return dot(projected, first_buf[0, span, :]) + dot(projected, first_buf[1, span, :])

    near, groups = 10, ny * CORES
    modal_buf[...] = modal_part(0, near)
    arrive_from(6, 4, 0, *lower)
    arrive_from(7, 4, 0, *upper)
    hand(17, 4)
    arrive_from(8, ny - 3, 0, *lower)
    hand(18, ny - 3, *lower)
    arrive_from(9, 3, 0, *upper)
    hand(19, 3, *upper)
    arrive_from(10, ny - 3, 0, *upper)
    hand(20, ny - 3, *upper)
    arrive_from(11, 3, 0, *lower)
    hand(21, 3, *lower)
    modal_buf[...] += modal_part(near, near + 3)
    arrive_from(17, 4, 1)
    arrive_from(18, ny - 3, 1, *lower)
    arrive_from(19, 3, 1, *upper)
    arrive_from(20, ny - 3, 1, *upper)
    arrive_from(21, 3, 1, *lower)
    modal = modal_buf[...] + modal_part(near + 3, groups)
    scale = jnp.concatenate([scale_buf[...]] * slots, axis=0)
    modal = (modal * scale).astype(BF16)
    solved = dot(modal, last_buf[0]) + dot(modal, last_buf[1])
    out_ref[...] = solved.reshape(slots, block, flat)

    for copy in copies + copies_z + pending:
        copy.wait_send()


def build(nx, nz, ny, slots, levels, trunc, lon, half, width):
    block = trunc // (ny * CORES)
    rows = slots * 6 * levels
    total_levels = levels * ny * CORES
    flat = 6 * total_levels
    lats = nx * nz * 2
    inner, units = lon // RADIX, trunc // RADIX
    cfg = dict(
        nx=nx, nz=nz, ny=ny, slots=slots, levels=levels, trunc=trunc, lon=lon, block=block,
        half=half,
    )
    dma = pltpu.SemaphoreType.DMA
    hbm = pl.BlockSpec(memory_space=pltpu.HBM)
    return pl.pallas_call(
        functools.partial(kernel, cfg),
        out_shape=jax.ShapeDtypeStruct((slots, block, flat), F32),
        in_specs=[hbm] * 8,
        out_specs=pl.BlockSpec(memory_space=pltpu.VMEM),
        scratch_shapes=[
            pltpu.VMEM((levels, 2, lon), BF16),
            pltpu.VMEM((levels, 2, lon), BF16),
            pltpu.VMEM((levels, 2, lon), BF16),
            pltpu.VMEM((trunc,), jnp.int32),
            pltpu.VMEM((total_levels, total_levels), F32),
            pltpu.VMEM((total_levels,), F32),
            pltpu.VMEM((RADIX // 2, 2 * inner, 8 * units), BF16),
            pltpu.VMEM((lats, width), BF16),
            pltpu.VMEM((lats, width), BF16),
            pltpu.VMEM((lats, width), BF16),
            pltpu.VMEM((lats, width), BF16),
            pltpu.VMEM((ny * CORES, rows, lats), BF16),
            pltpu.VMEM((slots, block, lats), BF16),
            pltpu.VMEM((slots * block, lats), F32),
            pltpu.VMEM((2, flat, flat), BF16),
            pltpu.VMEM((2, flat, flat), BF16),
            pltpu.VMEM((block, flat), F32),
            pltpu.VMEM((slots * block, flat), F32),
            dma((7,)), dma, dma((nx,)), dma((nx,)), dma((nz,)), dma((nz,)), dma((22,)), dma((22,)),
        ],
        compiler_params=pltpu.CompilerParams(
            collective_id=0, has_side_effects=True, vmem_limit_bytes=VMEM_LIMIT
        ),
    )


def body(humidity, wind_east, wind_north, legendre, owner, vertical_modes, mode_values):
    trunc = owner.shape[0]
    levels, pair, lon = humidity.shape
    owners = lax.axis_size("lat")
    nx, nz = split_lat(owners)
    ny = lax.axis_size("lev") // CORES
    slots = legendre.shape[0]
    rows = slots * 6 * levels
    half = -(-rows // 32) * 16
    width = -(-rows // 128) * 128
    table = fourier_table(lon, trunc // RADIX)
    high = table.astype(BF16)
    table = jnp.asarray(np.concatenate([high, (table - high.astype(np.float64)).astype(BF16)]))
    call = build(nx, nz, ny, slots, levels, trunc, lon, half, width)
    operands = [humidity, wind_east, wind_north, legendre, owner, vertical_modes, mode_values, table]
    return call(*[pltpu.with_memory_space_constraint(v, pltpu.HBM) for v in operands])


def solution(mesh):
    return jax.shard_map(
        body,
        mesh=mesh,
        in_specs=(
            P("lev", "lat", None),
            P("lev", "lat", None),
            P("lev", "lat", None),
            P("lat", None, None),
            P(),
            P(),
            P(),
        ),
        out_specs=P("lat", "lev", None),
        check_vma=False,
    )
```

```python
import functools
import math

import jax
import jax.numpy as jnp
import numpy as np
from jax import lax
from jax.experimental import pallas as pl
from jax.experimental.pallas import tpu as pltpu
from jax.sharding import PartitionSpec as P

MESH = pl.DeviceIdType.MESH
F32, BF16 = jnp.float32, jnp.bfloat16
RADIX = 20
CORES = 2
VMEM_LIMIT = 24 * 1024 * 1024


def split_lat(count):
    side = 1 << (int(math.log2(count)) // 2)
    return count // side, side


def lane_waves(units):
    rows = []
    for c in range(RADIX // 2):
        first, second = (0, RADIX // 2) if c == 0 else (c, RADIX - c)
        rows += [RADIX * u + first for u in range(units)] + [RADIX * u + second for u in range(units)]
    return np.array(rows)


def fourier_table(lon, units):
    inner = lon // RADIX
    waves = lane_waves(units).reshape(RADIX // 4, 4 * units)
    flip = np.ones((RADIX // 2, 2, units))
    flip[1:, 1] = -1.0
    flip = flip.reshape(RADIX // 4, 4 * units)
    phase = waves[:, None, :] * np.arange(inner)[None, :, None] % lon
    cos = np.cos(2 * np.pi * phase / lon) / math.sqrt(lon)
    sin = np.sin(2 * np.pi * phase / lon) / math.sqrt(lon)
    flip = flip[:, None, :]
    top = np.concatenate([cos, -sin], axis=2)
    bottom = np.concatenate([sin * flip, cos * flip], axis=2)
    return np.concatenate([top, bottom], axis=1)


def far_first(size):
    return sorted(range(1, size), key=lambda i: -min(i, size - i))


def place(rel, side):
    order = (0, 1, 7, 2, 6, 3, 5, 4).index(rel)
    return side * 5 + order if order < 5 else 10 + side * 3 + order - 5


def dot(a, b, contract=(1, 0)):
    return lax.dot_general(
        a, b, (((contract[0],), (contract[1],)), ((), ())), preferred_element_type=F32
    )


def iota(shape, axis):
    return lax.broadcasted_iota(jnp.int32, shape, axis)


def floor_div(value, divisor):
    return jnp.floor((value.astype(F32) + 0.5) * (1.0 / divisor))


def one_hot(mask):
    return jnp.where(mask, 1.0, 0.0).astype(BF16)


def short_fourier(x, inner):
    part = [x[:, inner * h : inner * (h + 1)] for h in range(RADIX)]
    half = RADIX // 2
    even = [part[h] + part[RADIX - h] for h in range(1, half)]
    odd = [part[h] - part[RADIX - h] for h in range(1, half)]
    real, imag = [None] * (half + 1), [None] * (half + 1)
    for q in range(half // 2 + 1):
        sums = []
        for parity in (0, 1):
            total = None
            for h in range(1, half):
                if h % 2 == parity:
                    factor = math.cos(2 * math.pi * ((q * h) % RADIX) / RADIX)
                    term = even[h - 1] * factor
                    total = term if total is None else total + term
            sums.append(total)
        ends_plus, ends_minus = part[0] + part[half], part[0] - part[half]
        first = sums[0] + (ends_plus if q % 2 == 0 else ends_minus)
        real[q] = first + sums[1]
        if q != half - q:
            other = sums[0] + (ends_plus if (half - q) % 2 == 0 else ends_minus)
            real[half - q] = other - sums[1]
    for q in range(half // 2 + 1):
        sums = []
        for parity in (0, 1):
            total = None
            for h in range(1, half):
                if h % 2 == parity:
                    factor = -math.sin(2 * math.pi * ((q * h) % RADIX) / RADIX)
                    term = odd[h - 1] * factor
                    total = term if total is None else total + term
            sums.append(total)
        imag[q] = sums[0] + sums[1]
        if q != half - q:
            imag[half - q] = sums[1] - sums[0]
    return real, imag


def kernel(
    cfg, hum_hbm, east_hbm, north_hbm, leg_ref, owner_hbm, modes_hbm, values_hbm, table_hbm,
    out_ref,
    hum_ref, east_ref, north_ref, owner_ref, modes_ref, values_ref, table_ref,
    out_buf, x_buf, z_send, z_buf, y_buf, leg_raw, leg_buf, first_buf, late_buf, last_buf, scale_buf,
    modal_buf,
    load_sem, leg_sem, x_send, x_recv, z_send_sem, z_recv, y_send, y_recv,
):
    nx, nz, ny, slots, levels, trunc, lon, block = (
        cfg[k] for k in ("nx", "nz", "ny", "slots", "levels", "trunc", "lon", "block")
    )
    lev, lat = lax.axis_index("lev"), lax.axis_index("lat")
    x, z = lat // nz, lat % nz
    y, core = lev // CORES, lev % CORES
    inner, units = lon // RADIX, trunc // RADIX
    fields = 3
    piece = 2 * fields * levels
    rows = slots * piece
    width = out_buf.shape[1]
    lats = nx * nz * 2
    total_levels = ny * CORES * levels
    flat = 2 * fields * total_levels
    bundle = 2 * nz
    bundle_z = 2 * nx

    def along_x(i):
        return {"lat": ((x + i) % nx) * nz + z}

    def along_z(i):
        return {"lat": x * nz + (z + i) % nz}

    def along_y(i):
        return {"lev": ((y + i) % ny) * CORES + core}

    partner = {"lev": y * CORES + 1 - core}

    loads = []
    for k, (source, target) in enumerate((
        (owner_hbm, owner_ref), (hum_hbm, hum_ref), (east_hbm, east_ref), (north_hbm, north_ref),
        (table_hbm, table_ref), (modes_hbm, modes_ref), (values_hbm, values_ref),
    )):
        loads.append(pltpu.make_async_copy(source, target, load_sem.at[k]))
        loads[-1].start()
    barrier = pltpu.get_barrier_semaphore()
    peers = [along_x(i) for i in far_first(nx)] + [along_z(i) for i in far_first(nz)]
    peers += [along_y(2), along_y(ny - 2), along_y(1), along_y(ny - 1), partner]
    for peer in peers:
        pl.semaphore_signal(barrier, inc=1, device_id=peer, device_id_type=MESH)
    leg_copy = pltpu.make_async_copy(
        leg_ref.at[:, pl.ds(pl.multiple_of(lev * block, 8), block), :], leg_raw, leg_sem
    )
    leg_copy.start()

    loads[0].wait()
    owner = owner_ref[...].reshape(1, trunc).astype(F32)
    owners = nx * nz
    member = owner == iota((owners, trunc), 0).astype(F32)
    before = one_hot(iota((trunc, trunc), 0) < iota((trunc, trunc), 1))
    count = dot(one_hot(member), before)
    rank = jnp.sum(jnp.where(member, count, 0.0), axis=0, keepdims=True)
    tall_slots = -(-slots // 8) * 8
    mine = (owner == lat.astype(F32)) & (rank == iota((tall_slots, trunc), 0).astype(F32))
    own_waves = jnp.sum(
        jnp.where(mine, iota((tall_slots, trunc), 1).astype(F32), 0.0), axis=1, keepdims=True
    )
    lane = iota((1, trunc), 1)
    clas = floor_div(lane, 2 * units)
    within = lane.astype(F32) - clas * (2 * units)
    second = within >= units
    unit = jnp.where(second, within - units, within)
    residue = jnp.where(second, jnp.where(clas == 0, RADIX // 2, RADIX - clas), clas)
    wave = RADIX * unit + residue
    reorder = one_hot(iota((trunc, trunc), 0).astype(F32) == wave)
    both = jnp.where(iota((16, trunc), 0) == 0, owner, jnp.where(iota((16, trunc), 0) == 1, rank, 0.0))
    both = dot(both.astype(BF16), reorder)
    owner_lane, rank_lane = both[0:1], both[1:2]

    for copy in loads[1:4]:
        copy.wait()
    humidity = hum_ref[...].astype(F32).reshape(2 * levels, lon)
    east = east_ref[...].astype(F32).reshape(2 * levels, lon)
    north = north_ref[...].astype(F32).reshape(2 * levels, lon)
    east = (east * humidity).astype(BF16).astype(F32)
    north = (north * humidity).astype(BF16).astype(F32)
    grid = jnp.concatenate([humidity, east, north], axis=0)
    real, imag = short_fourier(grid, inner)
    joined = [jnp.concatenate([r, i], axis=1) for r, i in zip(real, imag)]
    grid_rows = grid.shape[0]
    loads[4].wait()
    reals, imags = [], []
    for p in range(RADIX // 4):
        table = table_ref[p]
        if p == 0:
            left = jnp.concatenate([joined[0], joined[RADIX // 2], joined[1]], axis=0)
            limits = [units, 2 * units]
        else:
            left = jnp.concatenate([joined[2 * p], joined[2 * p + 1]], axis=0)
            limits = [2 * units]
        high = left.astype(BF16)
        low = (left - high.astype(F32)).astype(BF16)
        result = dot(high, table) + dot(low, table) + dot(high, table_ref[RADIX // 4 + p])
        column = iota((grid_rows, 8 * units), 1)
        column = jnp.where(column >= 4 * units, column - 4 * units, column)
        picked = result[len(limits) * grid_rows :]
        for k in reversed(range(len(limits))):
            picked = jnp.where(
                column < limits[k], result[k * grid_rows : (k + 1) * grid_rows], picked
            )
        reals.append(picked[:, : 4 * units])
        imags.append(picked[:, 4 * units :])
    spectrum = jnp.concatenate(
        [jnp.concatenate(reals, axis=1), jnp.concatenate(imags, axis=1)], axis=0
    ).astype(BF16)

    source = iota((piece, 2 * grid_rows), 1)
    target = iota((piece, 2 * grid_rows), 0)
    spread = []
    for t in range(2):
        pick = one_hot(2 * target + t == source)
        spread.append(dot(pick, spectrum))
    halves = []
    for t in range(2):
        pieces = [
            jnp.where(rank_lane == float(s), spread[t], 0.0) for s in range(slots)
        ] + [jnp.zeros((width - rows, trunc), F32)]
        halves.append(jnp.concatenate(pieces, axis=0))
    right = jnp.concatenate(halves, axis=1).astype(BF16)
    row = iota((2 * owners, trunc), 0).astype(F32)
    choose = jnp.concatenate(
        [
            jnp.where(2.0 * owner_lane == row, 1.0, 0.0),
            jnp.where(2.0 * owner_lane + 1.0 == row, 1.0, 0.0),
        ],
        axis=1,
    ).astype(BF16)
    out_buf[...] = dot(choose, right, (1, 1)).astype(BF16)

    pl.semaphore_wait(barrier, len(peers))

    copies = []
    for i in far_first(nx):
        to = (x + i) % nx
        copy = pltpu.make_async_remote_copy(
            src_ref=out_buf.at[pl.ds(pl.multiple_of(to * bundle, bundle), bundle)],
            dst_ref=x_buf.at[pl.ds(pl.multiple_of(x * bundle, bundle), bundle)],
            send_sem=x_send.at[i],
            recv_sem=x_recv.at[i],
            device_id=along_x(i),
            device_id_type=MESH,
        )
        copy.start()
        copies.append(copy)
    x_buf[pl.ds(pl.multiple_of(x * bundle, bundle), bundle), :] = out_buf[
        pl.ds(pl.multiple_of(x * bundle, bundle), bundle), :
    ]

    leg_copy.wait()
    arrive = iota((lats, lats), 1)
    from_z = arrive // bundle_z
    from_x = (arrive % bundle_z) // 2
    reach = one_hot(iota((lats, lats), 0) == (from_x * nz + from_z) * 2 + arrive % 2)
    leg = leg_raw[...].astype(F32).reshape(slots * block, lats).astype(BF16)
    leg = dot(leg, reach)
    degree = iota((block, lats), 0).astype(F32) + (lev * block).astype(F32)
    for s in range(slots):
        live = degree >= own_waves[s : s + 1, :]
        leg_buf[block * s : block * (s + 1), :] = jnp.where(
            live, leg[block * s : block * (s + 1)], 0.0
        )

    swap_to = iota((2 * owners, 2 * owners), 0)
    swap_from = iota((2 * owners, 2 * owners), 1)
    part_z, part_x, part_t = swap_to // bundle_z, (swap_to % bundle_z) // 2, swap_to % 2
    swap = one_hot(swap_from == part_x * bundle + part_z * 2 + part_t)

    loads[5].wait()
    loads[6].wait()
    modes = modes_ref[...]
    modes_high = modes.astype(BF16)
    modes_low = (modes - modes_high.astype(F32)).astype(BF16)
    tl = total_levels
    tile = one_hot(iota((tl, flat), 0) == (iota((tl, flat), 1) & (tl - 1)))
    column_part = iota((flat, flat), 1) // tl
    row_id = iota((flat, flat), 0)
    group = floor_div(row_id, piece)
    row_in = row_id.astype(F32) - group * piece
    row_part = floor_div(row_in, levels)
    id64 = iota((flat, tl), 0)
    group64 = floor_div(id64, piece)
    level64 = id64.astype(F32) - group64 * piece
    bases = [None] * (ny * CORES)
    for rel in range(ny):
        for side in range(CORES):
            level_group = ((y + rel) % ny) * CORES + (core if side == 0 else 1 - core)
            bases[place(rel, side)] = jnp.full(
                (piece, tl), (level_group * levels).astype(F32), F32
            )
    level64 = level64 - floor_div(level64, levels) * levels + jnp.concatenate(bases, axis=0)
    gather = one_hot(level64 == iota((flat, tl), 1).astype(F32))
    near, groups = 10, ny * CORES
    pair = 2 * tl
    late = (near + 3) * piece
    padded = late_buf.shape[0] // 2
    tile_pair = tile[:, :pair]
    same = iota((pair, pair), 0) // tl == iota((pair, pair), 1) // tl
    for k, part in enumerate((modes_high, modes_low)):
        stretched = dot(part, tile).astype(BF16)
        first = jnp.where(row_part == column_part.astype(F32), dot(gather, stretched), 0.0)
        first_buf[k] = first.astype(BF16)
        late_buf[k * padded : (k + 1) * padded, :] = jnp.concatenate(
            [first[late:], jnp.zeros((padded - flat + late, flat), F32)], axis=0
        ).astype(BF16)
        tall = dot(tile_pair, part, (0, 1)).astype(BF16)
        last_buf[k * pair : (k + 1) * pair, :] = jnp.where(
            same, dot(tall, tile_pair), 0.0
        ).astype(BF16)
    values = jnp.concatenate([values_ref[...].reshape(1, tl)] * (2 * fields), axis=1)
    number = iota((block, flat), 0).astype(F32) + (lev * block).astype(F32)
    shift = 4.0 * number * (number + 1.0) / (trunc * trunc)
    scale_buf[...] = 1.0 / (1.0 + shift * values)

    for copy in copies:
        copy.wait_recv()
    z_send[...] = dot(swap, x_buf[...]).astype(BF16)
    copies_z = []
    for i in far_first(nz):
        to = (z + i) % nz
        copy = pltpu.make_async_remote_copy(
            src_ref=z_send.at[pl.ds(pl.multiple_of(to * bundle_z, bundle_z), bundle_z)],
            dst_ref=z_buf.at[pl.ds(pl.multiple_of(z * bundle_z, bundle_z), bundle_z)],
            send_sem=z_send_sem.at[i],
            recv_sem=z_recv.at[i],
            device_id=along_z(i),
            device_id_type=MESH,
        )
        copy.start()
        copies_z.append(copy)
    z_buf[pl.ds(pl.multiple_of(z * bundle_z, bundle_z), bundle_z), :] = z_send[
        pl.ds(pl.multiple_of(z * bundle_z, bundle_z), bundle_z), :
    ]

    for copy in copies_z:
        copy.wait_recv()
    own = z_buf[...].astype(F32).T
    y_buf[place(0, 0)] = own[:rows].astype(BF16)

    pending = []
    half = cfg["half"]

    def message(k, rel, to, to_rel, side, start=0, size=rows):
        return pltpu.make_async_remote_copy(
            src_ref=y_buf.at[place(rel, 0), pl.ds(start, size)],
            dst_ref=y_buf.at[place(to_rel, side), pl.ds(start, size)],
            send_sem=y_send.at[k],
            recv_sem=y_recv.at[k],
            device_id=to,
            device_id_type=MESH,
        )

    def send(k, rel, step, start=0, size=rows):
        copy = message(k, rel, along_y(step % ny), (rel - step) % ny, 0, start, size)
        copy.start()
        return copy

    def relay(*args):
        pending.append(send(*args))

    def hand(k, rel, start=0, size=rows):
        copy = message(k, rel, partner, rel, 1, start, size)
        copy.start()
        pending.append(copy)

    def arrive_from(k, rel, side, start=0, size=rows):
        view = y_buf.at[place(rel, side), pl.ds(start, size)]
        pltpu.make_async_remote_copy(
            src_ref=view, dst_ref=view, send_sem=y_send.at[k], recv_sem=y_recv.at[k],
            device_id=partner, device_id_type=MESH,
        ).wait_recv()

    lower, upper = (0, half), (half, rows - half)
    below, above = ny - 2, 2
    for up, down in ((lower, upper), (upper, lower)):
        k = 0 if up == lower else 2
        first = send(k, 0, 2, *up), send(k + 1, 0, -2, *down)
        for copy in first:
            copy.wait_send()
    relay(4, 0, 1)
    relay(5, 0, -1)
    hand(12, 0)
    arrive_from(0, below, 0, *lower)
    relay(6, below, 2, *lower)
    relay(8, below, 1, *lower)
    arrive_from(1, above, 0, *upper)
    relay(7, above, -2, *upper)
    relay(9, above, -1, *upper)
    arrive_from(2, below, 0, *upper)
    relay(10, below, 1, *upper)
    arrive_from(3, above, 0, *lower)
    relay(11, above, -1, *lower)
    hand(13, below)
    hand(14, above)
    arrive_from(4, ny - 1, 0)
    hand(15, ny - 1)
    arrive_from(5, 1, 0)
    hand(16, 1)
    arrive_from(12, 0, 1)
    arrive_from(13, below, 1)
    arrive_from(14, above, 1)
    arrive_from(15, ny - 1, 1)
    arrive_from(16, 1, 1)

    def project(first, last, padding):
        pieces = []
        for s in range(slots):
            blocks = [y_buf[g, piece * s : piece * (s + 1), :] for g in range(first, last)]
            if padding:
                blocks.append(jnp.zeros((padding, lats), BF16))
            left = leg_buf[block * s : block * (s + 1), :].astype(BF16)
            pieces.append(dot(left, jnp.concatenate(blocks, axis=0), (1, 1)))
        return jnp.concatenate(pieces, axis=0).astype(BF16)

    def modal_part(first, last):
        projected = project(first, last, 0)
        span = slice(first * piece, last * piece)
        return dot(projected, first_buf[0, span, :]) + dot(projected, first_buf[1, span, :])

    modal_buf[...] = modal_part(0, near)
    arrive_from(6, 4, 0, *lower)
    arrive_from(7, 4, 0, *upper)
    hand(17, 4)
    arrive_from(8, ny - 3, 0, *lower)
    hand(18, ny - 3, *lower)
    arrive_from(9, 3, 0, *upper)
    hand(19, 3, *upper)
    arrive_from(10, ny - 3, 0, *upper)
    hand(20, ny - 3, *upper)
    arrive_from(11, 3, 0, *lower)
    hand(21, 3, *lower)
    modal_buf[...] += modal_part(near, near + 3)
    arrive_from(17, 4, 1)
    arrive_from(18, ny - 3, 1, *lower)
    arrive_from(19, 3, 1, *upper)
    arrive_from(20, ny - 3, 1, *upper)
    arrive_from(21, 3, 1, *lower)
    projected = project(near + 3, groups, padded - flat + late)
    modal = modal_buf[...] + dot(jnp.concatenate([projected, projected], axis=1), late_buf[...])
    scale = jnp.concatenate([scale_buf[...]] * slots, axis=0)
    modal = (modal * scale).astype(BF16)
    solved = []
    for j in range(flat // pair):
        part = modal[:, j * pair : (j + 1) * pair]
        solved.append(dot(jnp.concatenate([part, part], axis=1), last_buf[...]))
    solved = jnp.concatenate(solved, axis=1)
    out_ref[...] = solved.reshape(slots, block, flat)

    for copy in copies + copies_z + pending:
        copy.wait_send()


def build(nx, nz, ny, slots, levels, trunc, lon, half, width):
    block = trunc // (ny * CORES)
    rows = slots * 6 * levels
    total_levels = levels * ny * CORES
    flat = 6 * total_levels
    lats = nx * nz * 2
    inner, units = lon // RADIX, trunc // RADIX
    cfg = dict(
        nx=nx, nz=nz, ny=ny, slots=slots, levels=levels, trunc=trunc, lon=lon, block=block,
        half=half,
    )
    dma = pltpu.SemaphoreType.DMA
    hbm = pl.BlockSpec(memory_space=pltpu.HBM)
    return pl.pallas_call(
        functools.partial(kernel, cfg),
        out_shape=jax.ShapeDtypeStruct((slots, block, flat), F32),
        in_specs=[hbm] * 8,
        out_specs=pl.BlockSpec(memory_space=pltpu.VMEM),
        scratch_shapes=[
            pltpu.VMEM((levels, 2, lon), BF16),
            pltpu.VMEM((levels, 2, lon), BF16),
            pltpu.VMEM((levels, 2, lon), BF16),
            pltpu.VMEM((trunc,), jnp.int32),
            pltpu.VMEM((total_levels, total_levels), F32),
            pltpu.VMEM((total_levels,), F32),
            pltpu.VMEM((RADIX // 2, 2 * inner, 8 * units), BF16),
            pltpu.VMEM((lats, width), BF16),
            pltpu.VMEM((lats, width), BF16),
            pltpu.VMEM((lats, width), BF16),
            pltpu.VMEM((lats, width), BF16),
            pltpu.VMEM((ny * CORES, rows, lats), BF16),
            pltpu.VMEM((slots, block, lats), BF16),
            pltpu.VMEM((slots * block, lats), F32),
            pltpu.VMEM((2, flat, flat), BF16),
            pltpu.VMEM((2 * (-(-18 * levels // 128) * 128), flat), BF16),
            pltpu.VMEM((4 * total_levels, 2 * total_levels), BF16),
            pltpu.VMEM((block, flat), F32),
            pltpu.VMEM((slots * block, flat), F32),
            dma((7,)), dma, dma((nx,)), dma((nx,)), dma((nz,)), dma((nz,)), dma((22,)), dma((22,)),
        ],
        compiler_params=pltpu.CompilerParams(
            collective_id=0, has_side_effects=True, vmem_limit_bytes=VMEM_LIMIT
        ),
    )


def body(humidity, wind_east, wind_north, legendre, owner, vertical_modes, mode_values):
    trunc = owner.shape[0]
    levels, pair, lon = humidity.shape
    owners = lax.axis_size("lat")
    nx, nz = split_lat(owners)
    ny = lax.axis_size("lev") // CORES
    slots = legendre.shape[0]
    rows = slots * 6 * levels
    half = -(-rows // 32) * 16
    width = -(-rows // 128) * 128
    table = fourier_table(lon, trunc // RADIX)
    high = table.astype(BF16)
    table = jnp.asarray(np.concatenate([high, (table - high.astype(np.float64)).astype(BF16)]))
    call = build(nx, nz, ny, slots, levels, trunc, lon, half, width)
    operands = [humidity, wind_east, wind_north, legendre, owner, vertical_modes, mode_values, table]
    return call(*[pltpu.with_memory_space_constraint(v, pltpu.HBM) for v in operands])


def solution(mesh):
    return jax.shard_map(
        body,
        mesh=mesh,
        in_specs=(
            P("lev", "lat", None),
            P("lev", "lat", None),
            P("lev", "lat", None),
            P("lat", None, None),
            P(),
            P(),
            P(),
        ),
        out_specs=P("lat", "lev", None),
        check_vma=False,
    )
```

```python
import functools
import math

import jax
import jax.numpy as jnp
import numpy as np
from jax import lax
from jax.experimental import pallas as pl
from jax.experimental.pallas import tpu as pltpu
from jax.sharding import PartitionSpec as P

MESH = pl.DeviceIdType.MESH
F32, BF16 = jnp.float32, jnp.bfloat16
RADIX = 20
CORES = 2
VMEM_LIMIT = 24 * 1024 * 1024


def split_lat(count):
    side = 1 << (int(math.log2(count)) // 2)
    return count // side, side


def lane_waves(units):
    rows = []
    for c in range(RADIX // 2):
        first, second = (0, RADIX // 2) if c == 0 else (c, RADIX - c)
        rows += [RADIX * u + first for u in range(units)] + [RADIX * u + second for u in range(units)]
    return np.array(rows)


def fourier_table(lon, units):
    inner = lon // RADIX
    waves = lane_waves(units).reshape(RADIX // 4, 4 * units)
    flip = np.ones((RADIX // 2, 2, units))
    flip[1:, 1] = -1.0
    flip = flip.reshape(RADIX // 4, 4 * units)
    phase = waves[:, None, :] * np.arange(inner)[None, :, None] % lon
    cos = np.cos(2 * np.pi * phase / lon) / math.sqrt(lon)
    sin = np.sin(2 * np.pi * phase / lon) / math.sqrt(lon)
    flip = flip[:, None, :]
    top = np.concatenate([cos, -sin], axis=2)
    bottom = np.concatenate([sin * flip, cos * flip], axis=2)
    return np.concatenate([top, bottom], axis=1)


def far_first(size):
    return sorted(range(1, size), key=lambda i: -min(i, size - i))


def place(rel, side):
    order = (0, 1, 7, 2, 6, 3, 5, 4).index(rel)
    return side * 5 + order if order < 5 else 10 + side * 3 + order - 5


def dot(a, b, contract=(1, 0)):
    return lax.dot_general(
        a, b, (((contract[0],), (contract[1],)), ((), ())), preferred_element_type=F32
    )


def iota(shape, axis):
    return lax.broadcasted_iota(jnp.int32, shape, axis)


def floor_div(value, divisor):
    return jnp.floor((value.astype(F32) + 0.5) * (1.0 / divisor))


def one_hot(mask):
    return jnp.where(mask, 1.0, 0.0).astype(BF16)


def short_fourier(x, inner):
    part = [x[:, inner * h : inner * (h + 1)] for h in range(RADIX)]
    half = RADIX // 2
    even = [part[h] + part[RADIX - h] for h in range(1, half)]
    odd = [part[h] - part[RADIX - h] for h in range(1, half)]
    real, imag = [None] * (half + 1), [None] * (half + 1)
    for q in range(half // 2 + 1):
        sums = []
        for parity in (0, 1):
            total = None
            for h in range(1, half):
                if h % 2 == parity:
                    factor = math.cos(2 * math.pi * ((q * h) % RADIX) / RADIX)
                    term = even[h - 1] * factor
                    total = term if total is None else total + term
            sums.append(total)
        ends_plus, ends_minus = part[0] + part[half], part[0] - part[half]
        first = sums[0] + (ends_plus if q % 2 == 0 else ends_minus)
        real[q] = first + sums[1]
        if q != half - q:
            other = sums[0] + (ends_plus if (half - q) % 2 == 0 else ends_minus)
            real[half - q] = other - sums[1]
    for q in range(half // 2 + 1):
        sums = []
        for parity in (0, 1):
            total = None
            for h in range(1, half):
                if h % 2 == parity:
                    factor = -math.sin(2 * math.pi * ((q * h) % RADIX) / RADIX)
                    term = odd[h - 1] * factor
                    total = term if total is None else total + term
            sums.append(total)
        imag[q] = sums[0] + sums[1]
        if q != half - q:
            imag[half - q] = sums[1] - sums[0]
    return real, imag


def kernel(
    cfg, hum_hbm, east_hbm, north_hbm, leg_ref, owner_hbm, modes_hbm, values_hbm, table_hbm,
    out_ref,
    hum_ref, east_ref, north_ref, owner_ref, modes_ref, values_ref, table_ref,
    out_buf, x_buf, z_send, z_buf, y_buf, leg_raw, leg_buf, first_buf, late_buf, last_buf, scale_buf,
    modal_buf,
    load_sem, leg_sem, x_send, x_recv, z_send_sem, z_recv, y_send, y_recv,
):
    nx, nz, ny, slots, levels, trunc, lon, block = (
        cfg[k] for k in ("nx", "nz", "ny", "slots", "levels", "trunc", "lon", "block")
    )
    lev, lat = lax.axis_index("lev"), lax.axis_index("lat")
    x, z = lat // nz, lat % nz
    y, core = lev // CORES, lev % CORES
    inner, units = lon // RADIX, trunc // RADIX
    fields = 3
    piece = 2 * fields * levels
    rows = slots * piece
    width = out_buf.shape[1]
    lats = nx * nz * 2
    total_levels = ny * CORES * levels
    flat = 2 * fields * total_levels
    bundle = 2 * nz
    bundle_z = 2 * nx

    def along_x(i):
        return {"lat": ((x + i) % nx) * nz + z}

    def along_z(i):
        return {"lat": x * nz + (z + i) % nz}

    def along_y(i):
        return {"lev": ((y + i) % ny) * CORES + core}

    partner = {"lev": y * CORES + 1 - core}

    barrier = pltpu.get_barrier_semaphore()
    peers = [along_x(i) for i in far_first(nx)] + [along_z(i) for i in far_first(nz)]
    peers += [along_y(2), along_y(ny - 2), along_y(1), along_y(ny - 1), partner]
    for peer in peers:
        pl.semaphore_signal(barrier, inc=1, device_id=peer, device_id_type=MESH)
    loads = []
    for k, (source, target) in enumerate((
        (owner_hbm, owner_ref), (hum_hbm, hum_ref), (east_hbm, east_ref), (north_hbm, north_ref),
        (table_hbm, table_ref), (modes_hbm, modes_ref), (values_hbm, values_ref),
    )):
        loads.append(pltpu.make_async_copy(source, target, load_sem.at[k]))
        loads[-1].start()
    leg_copy = pltpu.make_async_copy(
        leg_ref.at[:, pl.ds(pl.multiple_of(lev * block, 8), block), :], leg_raw, leg_sem
    )
    leg_copy.start()

    loads[0].wait()
    owner = owner_ref[...].reshape(1, trunc).astype(F32)
    owners = nx * nz
    member = owner == iota((owners, trunc), 0).astype(F32)
    before = one_hot(iota((trunc, trunc), 0) < iota((trunc, trunc), 1))
    count = dot(one_hot(member), before)
    rank = jnp.sum(jnp.where(member, count, 0.0), axis=0, keepdims=True)
    tall_slots = -(-slots // 8) * 8
    mine = (owner == lat.astype(F32)) & (rank == iota((tall_slots, trunc), 0).astype(F32))
    own_waves = jnp.sum(
        jnp.where(mine, iota((tall_slots, trunc), 1).astype(F32), 0.0), axis=1, keepdims=True
    )
    lane = iota((1, trunc), 1)
    clas = floor_div(lane, 2 * units)
    within = lane.astype(F32) - clas * (2 * units)
    second = within >= units
    unit = jnp.where(second, within - units, within)
    residue = jnp.where(second, jnp.where(clas == 0, RADIX // 2, RADIX - clas), clas)
    wave = RADIX * unit + residue
    reorder = one_hot(iota((trunc, trunc), 0).astype(F32) == wave)
    both = jnp.where(iota((16, trunc), 0) == 0, owner, jnp.where(iota((16, trunc), 0) == 1, rank, 0.0))
    both = dot(both.astype(BF16), reorder)
    owner_lane, rank_lane = both[0:1], both[1:2]

    for copy in loads[1:4]:
        copy.wait()
    humidity = hum_ref[...].astype(F32).reshape(2 * levels, lon)
    east = east_ref[...].astype(F32).reshape(2 * levels, lon)
    north = north_ref[...].astype(F32).reshape(2 * levels, lon)
    east = (east * humidity).astype(BF16).astype(F32)
    north = (north * humidity).astype(BF16).astype(F32)
    grid = jnp.concatenate([humidity, east, north], axis=0)
    real, imag = short_fourier(grid, inner)
    joined = [jnp.concatenate([r, i], axis=1) for r, i in zip(real, imag)]
    grid_rows = grid.shape[0]
    loads[4].wait()
    reals, imags = [], []
    for p in range(RADIX // 4):
        table = table_ref[p]
        if p == 0:
            left = jnp.concatenate([joined[0], joined[RADIX // 2], joined[1]], axis=0)
            limits = [units, 2 * units]
        else:
            left = jnp.concatenate([joined[2 * p], joined[2 * p + 1]], axis=0)
            limits = [2 * units]
        high = left.astype(BF16)
        low = (left - high.astype(F32)).astype(BF16)
        result = dot(high, table) + dot(low, table) + dot(high, table_ref[RADIX // 4 + p])
        column = iota((grid_rows, 8 * units), 1)
        column = jnp.where(column >= 4 * units, column - 4 * units, column)
        picked = result[len(limits) * grid_rows :]
        for k in reversed(range(len(limits))):
            picked = jnp.where(
                column < limits[k], result[k * grid_rows : (k + 1) * grid_rows], picked
            )
        reals.append(picked[:, : 4 * units])
        imags.append(picked[:, 4 * units :])
    spectrum = jnp.concatenate(
        [jnp.concatenate(reals, axis=1), jnp.concatenate(imags, axis=1)], axis=0
    ).astype(BF16)

    source = iota((piece, 2 * grid_rows), 1)
    target = iota((piece, 2 * grid_rows), 0)
    spread = []
    for t in range(2):
        pick = one_hot(2 * target + t == source)
        spread.append(dot(pick, spectrum))
    halves = []
    for t in range(2):
        pieces = [
            jnp.where(rank_lane == float(s), spread[t], 0.0) for s in range(slots)
        ] + [jnp.zeros((width - rows, trunc), F32)]
        halves.append(jnp.concatenate(pieces, axis=0))
    right = jnp.concatenate(halves, axis=1).astype(BF16)
    row = iota((2 * owners, trunc), 0).astype(F32)
    choose = jnp.concatenate(
        [
            jnp.where(2.0 * owner_lane == row, 1.0, 0.0),
            jnp.where(2.0 * owner_lane + 1.0 == row, 1.0, 0.0),
        ],
        axis=1,
    ).astype(BF16)
    out_buf[...] = dot(choose, right, (1, 1)).astype(BF16)

    pl.semaphore_wait(barrier, len(peers))

    copies = []
    for i in far_first(nx):
        to = (x + i) % nx
        copy = pltpu.make_async_remote_copy(
            src_ref=out_buf.at[pl.ds(pl.multiple_of(to * bundle, bundle), bundle)],
            dst_ref=x_buf.at[pl.ds(pl.multiple_of(x * bundle, bundle), bundle)],
            send_sem=x_send.at[i],
            recv_sem=x_recv.at[i],
            device_id=along_x(i),
            device_id_type=MESH,
        )
        copy.start()
        copies.append(copy)
    x_buf[pl.ds(pl.multiple_of(x * bundle, bundle), bundle), :] = out_buf[
        pl.ds(pl.multiple_of(x * bundle, bundle), bundle), :
    ]

    leg_copy.wait()
    arrive = iota((lats, lats), 1)
    from_z = arrive // bundle_z
    from_x = (arrive % bundle_z) // 2
    reach = one_hot(iota((lats, lats), 0) == (from_x * nz + from_z) * 2 + arrive % 2)
    leg = leg_raw[...].astype(F32).reshape(slots * block, lats).astype(BF16)
    leg = dot(leg, reach)
    degree = iota((block, lats), 0).astype(F32) + (lev * block).astype(F32)
    for s in range(slots):
        live = degree >= own_waves[s : s + 1, :]
        leg_buf[block * s : block * (s + 1), :] = jnp.where(
            live, leg[block * s : block * (s + 1)], 0.0
        )

    swap_to = iota((2 * owners, 2 * owners), 0)
    swap_from = iota((2 * owners, 2 * owners), 1)
    part_z, part_x, part_t = swap_to // bundle_z, (swap_to % bundle_z) // 2, swap_to % 2
    swap = one_hot(swap_from == part_x * bundle + part_z * 2 + part_t)

    loads[5].wait()
    loads[6].wait()
    modes = modes_ref[...]
    modes_high = modes.astype(BF16)
    modes_low = (modes - modes_high.astype(F32)).astype(BF16)
    tl = total_levels
    tile = one_hot(iota((tl, flat), 0) == (iota((tl, flat), 1) & (tl - 1)))
    column_part = iota((flat, flat), 1) // tl
    row_id = iota((flat, flat), 0)
    group = floor_div(row_id, piece)
    row_in = row_id.astype(F32) - group * piece
    row_part = floor_div(row_in, levels)
    id64 = iota((flat, tl), 0)
    group64 = floor_div(id64, piece)
    level64 = id64.astype(F32) - group64 * piece
    bases = [None] * (ny * CORES)
    for rel in range(ny):
        for side in range(CORES):
            level_group = ((y + rel) % ny) * CORES + (core if side == 0 else 1 - core)
            bases[place(rel, side)] = jnp.full(
                (piece, tl), (level_group * levels).astype(F32), F32
            )
    level64 = level64 - floor_div(level64, levels) * levels + jnp.concatenate(bases, axis=0)
    gather = one_hot(level64 == iota((flat, tl), 1).astype(F32))
    near, groups = 10, ny * CORES
    pair = 2 * tl
    late = (near + 3) * piece
    padded = late_buf.shape[0] // 2
    tile_pair = tile[:, :pair]
    same = iota((pair, pair), 0) // tl == iota((pair, pair), 1) // tl
    for k, part in enumerate((modes_high, modes_low)):
        stretched = dot(part, tile).astype(BF16)
        first = jnp.where(row_part == column_part.astype(F32), dot(gather, stretched), 0.0)
        first_buf[k] = first.astype(BF16)
        late_buf[k * padded : (k + 1) * padded, :] = jnp.concatenate(
            [first[late:], jnp.zeros((padded - flat + late, flat), F32)], axis=0
        ).astype(BF16)
        tall = dot(tile_pair, part, (0, 1)).astype(BF16)
        last_buf[k * pair : (k + 1) * pair, :] = jnp.where(
            same, dot(tall, tile_pair), 0.0
        ).astype(BF16)
    values = jnp.concatenate([values_ref[...].reshape(1, tl)] * (2 * fields), axis=1)
    number = iota((block, flat), 0).astype(F32) + (lev * block).astype(F32)
    shift = 4.0 * number * (number + 1.0) / (trunc * trunc)
    scale_buf[...] = 1.0 / (1.0 + shift * values)

    for copy in copies:
        copy.wait_recv()
    z_send[...] = dot(swap, x_buf[...]).astype(BF16)
    copies_z = []
    for i in far_first(nz):
        to = (z + i) % nz
        copy = pltpu.make_async_remote_copy(
            src_ref=z_send.at[pl.ds(pl.multiple_of(to * bundle_z, bundle_z), bundle_z)],
            dst_ref=z_buf.at[pl.ds(pl.multiple_of(z * bundle_z, bundle_z), bundle_z)],
            send_sem=z_send_sem.at[i],
            recv_sem=z_recv.at[i],
            device_id=along_z(i),
            device_id_type=MESH,
        )
        copy.start()
        copies_z.append(copy)
    z_buf[pl.ds(pl.multiple_of(z * bundle_z, bundle_z), bundle_z), :] = z_send[
        pl.ds(pl.multiple_of(z * bundle_z, bundle_z), bundle_z), :
    ]

    for copy in copies_z:
        copy.wait_recv()
    own = z_buf[...].astype(F32).T
    y_buf[place(0, 0)] = own[:rows].astype(BF16)

    pending = []
    half = cfg["half"]

    def message(k, rel, to, to_rel, side, start=0, size=rows):
        return pltpu.make_async_remote_copy(
            src_ref=y_buf.at[place(rel, 0), pl.ds(start, size)],
            dst_ref=y_buf.at[place(to_rel, side), pl.ds(start, size)],
            send_sem=y_send.at[k],
            recv_sem=y_recv.at[k],
            device_id=to,
            device_id_type=MESH,
        )

    def send(k, rel, step, start=0, size=rows):
        copy = message(k, rel, along_y(step % ny), (rel - step) % ny, 0, start, size)
        copy.start()
        return copy

    def relay(*args):
        pending.append(send(*args))

    def hand(k, rel, start=0, size=rows):
        copy = message(k, rel, partner, rel, 1, start, size)
        copy.start()
        pending.append(copy)

    def arrive_from(k, rel, side, start=0, size=rows):
        view = y_buf.at[place(rel, side), pl.ds(start, size)]
        pltpu.make_async_remote_copy(
            src_ref=view, dst_ref=view, send_sem=y_send.at[k], recv_sem=y_recv.at[k],
            device_id=partner, device_id_type=MESH,
        ).wait_recv()

    lower, upper = (0, half), (half, rows - half)
    below, above = ny - 2, 2
    relay(0, 0, 2, *lower)
    relay(1, 0, -2, *upper)
    relay(2, 0, 2, *upper)
    relay(3, 0, -2, *lower)
    relay(4, 0, 1)
    relay(5, 0, -1)
    hand(12, 0)
    arrive_from(0, below, 0, *lower)
    relay(6, below, 2, *lower)
    relay(8, below, 1, *lower)
    arrive_from(1, above, 0, *upper)
    relay(7, above, -2, *upper)
    relay(9, above, -1, *upper)
    arrive_from(2, below, 0, *upper)
    relay(10, below, 1, *upper)
    arrive_from(3, above, 0, *lower)
    relay(11, above, -1, *lower)
    hand(13, below)
    hand(14, above)
    arrive_from(4, ny - 1, 0)
    hand(15, ny - 1)
    arrive_from(5, 1, 0)
    hand(16, 1)
    arrive_from(12, 0, 1)
    arrive_from(13, below, 1)
    arrive_from(14, above, 1)
    arrive_from(15, ny - 1, 1)
    arrive_from(16, 1, 1)

    def project(first, last, padding):
        pieces = []
        for s in range(slots):
            blocks = [y_buf[g, piece * s : piece * (s + 1), :] for g in range(first, last)]
            if padding:
                blocks.append(jnp.zeros((padding, lats), BF16))
            left = leg_buf[block * s : block * (s + 1), :].astype(BF16)
            pieces.append(dot(left, jnp.concatenate(blocks, axis=0), (1, 1)))
        return jnp.concatenate(pieces, axis=0).astype(BF16)

    def modal_part(first, last):
        projected = project(first, last, 0)
        span = slice(first * piece, last * piece)
        return dot(projected, first_buf[0, span, :]) + dot(projected, first_buf[1, span, :])

    modal_buf[...] = modal_part(0, near)
    arrive_from(8, ny - 3, 0, *lower)
    hand(18, ny - 3, *lower)
    arrive_from(9, 3, 0, *upper)
    hand(19, 3, *upper)
    arrive_from(6, 4, 0, *lower)
    arrive_from(7, 4, 0, *upper)
    hand(17, 4)
    arrive_from(10, ny - 3, 0, *upper)
    hand(20, ny - 3, *upper)
    arrive_from(11, 3, 0, *lower)
    hand(21, 3, *lower)
    modal_buf[...] += modal_part(near, near + 3)
    arrive_from(17, 4, 1)
    arrive_from(18, ny - 3, 1, *lower)
    arrive_from(19, 3, 1, *upper)
    arrive_from(20, ny - 3, 1, *upper)
    arrive_from(21, 3, 1, *lower)
    projected = project(near + 3, groups, padded - flat + late)
    modal = modal_buf[...] + dot(jnp.concatenate([projected, projected], axis=1), late_buf[...])
    scale = jnp.concatenate([scale_buf[...]] * slots, axis=0)
    modal = (modal * scale).astype(BF16)
    solved = []
    for j in range(flat // pair):
        part = modal[:, j * pair : (j + 1) * pair]
        solved.append(dot(jnp.concatenate([part, part], axis=1), last_buf[...]))
    solved = jnp.concatenate(solved, axis=1)
    out_ref[...] = solved.reshape(slots, block, flat)

    for copy in copies + copies_z + pending:
        copy.wait_send()


def build(nx, nz, ny, slots, levels, trunc, lon, half, width):
    block = trunc // (ny * CORES)
    rows = slots * 6 * levels
    total_levels = levels * ny * CORES
    flat = 6 * total_levels
    lats = nx * nz * 2
    inner, units = lon // RADIX, trunc // RADIX
    cfg = dict(
        nx=nx, nz=nz, ny=ny, slots=slots, levels=levels, trunc=trunc, lon=lon, block=block,
        half=half,
    )
    dma = pltpu.SemaphoreType.DMA
    hbm = pl.BlockSpec(memory_space=pltpu.HBM)
    return pl.pallas_call(
        functools.partial(kernel, cfg),
        out_shape=jax.ShapeDtypeStruct((slots, block, flat), F32),
        in_specs=[hbm] * 8,
        out_specs=pl.BlockSpec(memory_space=pltpu.VMEM),
        scratch_shapes=[
            pltpu.VMEM((levels, 2, lon), BF16),
            pltpu.VMEM((levels, 2, lon), BF16),
            pltpu.VMEM((levels, 2, lon), BF16),
            pltpu.VMEM((trunc,), jnp.int32),
            pltpu.VMEM((total_levels, total_levels), F32),
            pltpu.VMEM((total_levels,), F32),
            pltpu.VMEM((RADIX // 2, 2 * inner, 8 * units), BF16),
            pltpu.VMEM((lats, width), BF16),
            pltpu.VMEM((lats, width), BF16),
            pltpu.VMEM((lats, width), BF16),
            pltpu.VMEM((lats, width), BF16),
            pltpu.VMEM((ny * CORES, rows, lats), BF16),
            pltpu.VMEM((slots, block, lats), BF16),
            pltpu.VMEM((slots * block, lats), F32),
            pltpu.VMEM((2, flat, flat), BF16),
            pltpu.VMEM((2 * (-(-18 * levels // 128) * 128), flat), BF16),
            pltpu.VMEM((4 * total_levels, 2 * total_levels), BF16),
            pltpu.VMEM((block, flat), F32),
            pltpu.VMEM((slots * block, flat), F32),
            dma((7,)), dma, dma((nx,)), dma((nx,)), dma((nz,)), dma((nz,)), dma((22,)), dma((22,)),
        ],
        compiler_params=pltpu.CompilerParams(
            collective_id=0, has_side_effects=True, vmem_limit_bytes=VMEM_LIMIT
        ),
    )


def body(humidity, wind_east, wind_north, legendre, owner, vertical_modes, mode_values):
    trunc = owner.shape[0]
    levels, pair, lon = humidity.shape
    owners = lax.axis_size("lat")
    nx, nz = split_lat(owners)
    ny = lax.axis_size("lev") // CORES
    slots = legendre.shape[0]
    rows = slots * 6 * levels
    half = -(-rows // 32) * 16
    width = -(-rows // 128) * 128
    table = fourier_table(lon, trunc // RADIX)
    high = table.astype(BF16)
    table = jnp.asarray(np.concatenate([high, (table - high.astype(np.float64)).astype(BF16)]))
    call = build(nx, nz, ny, slots, levels, trunc, lon, half, width)
    operands = [humidity, wind_east, wind_north, legendre, owner, vertical_modes, mode_values, table]
    return call(*[pltpu.with_memory_space_constraint(v, pltpu.HBM) for v in operands])


def solution(mesh):
    return jax.shard_map(
        body,
        mesh=mesh,
        in_specs=(
            P("lev", "lat", None),
            P("lev", "lat", None),
            P("lev", "lat", None),
            P("lat", None, None),
            P(),
            P(),
            P(),
        ),
        out_specs=P("lat", "lev", None),
        check_vma=False,
    )
```

```python
import functools
import math

import jax
import jax.numpy as jnp
import numpy as np
from jax import lax
from jax.experimental import pallas as pl
from jax.experimental.pallas import tpu as pltpu
from jax.sharding import PartitionSpec as P

MESH = pl.DeviceIdType.MESH
F32, BF16 = jnp.float32, jnp.bfloat16
RADIX = 20
CORES = 2
VMEM_LIMIT = 24 * 1024 * 1024


def split_lat(count):
    side = 1 << (int(math.log2(count)) // 2)
    return count // side, side


def lane_waves(units):
    rows = []
    for c in range(RADIX // 2):
        first, second = (0, RADIX // 2) if c == 0 else (c, RADIX - c)
        rows += [RADIX * u + first for u in range(units)] + [RADIX * u + second for u in range(units)]
    return np.array(rows)


def fourier_table(lon, units):
    inner = lon // RADIX
    waves = lane_waves(units).reshape(RADIX // 4, 4 * units)
    flip = np.ones((RADIX // 2, 2, units))
    flip[1:, 1] = -1.0
    flip = flip.reshape(RADIX // 4, 4 * units)
    phase = waves[:, None, :] * np.arange(inner)[None, :, None] % lon
    cos = np.cos(2 * np.pi * phase / lon) / math.sqrt(lon)
    sin = np.sin(2 * np.pi * phase / lon) / math.sqrt(lon)
    flip = flip[:, None, :]
    top = np.concatenate([cos, -sin], axis=2)
    bottom = np.concatenate([sin * flip, cos * flip], axis=2)
    return np.concatenate([top, bottom], axis=1)


def far_first(size):
    return sorted(range(1, size), key=lambda i: -min(i, size - i))


def place(rel, side):
    order = (0, 1, 7, 2, 6, 3, 5, 4).index(rel)
    return side * 5 + order if order < 5 else 10 + side * 3 + order - 5


def dot(a, b, contract=(1, 0)):
    return lax.dot_general(
        a, b, (((contract[0],), (contract[1],)), ((), ())), preferred_element_type=F32
    )


def iota(shape, axis):
    return lax.broadcasted_iota(jnp.int32, shape, axis)


def floor_div(value, divisor):
    return jnp.floor((value.astype(F32) + 0.5) * (1.0 / divisor))


def one_hot(mask):
    return jnp.where(mask, 1.0, 0.0).astype(BF16)


def short_fourier(x, inner):
    part = [x[:, inner * h : inner * (h + 1)] for h in range(RADIX)]
    half = RADIX // 2
    even = [part[h] + part[RADIX - h] for h in range(1, half)]
    odd = [part[h] - part[RADIX - h] for h in range(1, half)]
    real, imag = [None] * (half + 1), [None] * (half + 1)
    for q in range(half // 2 + 1):
        sums = []
        for parity in (0, 1):
            total = None
            for h in range(1, half):
                if h % 2 == parity:
                    factor = math.cos(2 * math.pi * ((q * h) % RADIX) / RADIX)
                    term = even[h - 1] * factor
                    total = term if total is None else total + term
            sums.append(total)
        ends_plus, ends_minus = part[0] + part[half], part[0] - part[half]
        first = sums[0] + (ends_plus if q % 2 == 0 else ends_minus)
        real[q] = first + sums[1]
        if q != half - q:
            other = sums[0] + (ends_plus if (half - q) % 2 == 0 else ends_minus)
            real[half - q] = other - sums[1]
    for q in range(half // 2 + 1):
        sums = []
        for parity in (0, 1):
            total = None
            for h in range(1, half):
                if h % 2 == parity:
                    factor = -math.sin(2 * math.pi * ((q * h) % RADIX) / RADIX)
                    term = odd[h - 1] * factor
                    total = term if total is None else total + term
            sums.append(total)
        imag[q] = sums[0] + sums[1]
        if q != half - q:
            imag[half - q] = sums[1] - sums[0]
    return real, imag


def kernel(
    cfg, hum_hbm, east_hbm, north_hbm, leg_ref, owner_hbm, modes_hbm, values_hbm, table_hbm,
    out_ref,
    hum_ref, east_ref, north_ref, owner_ref, modes_ref, values_ref, table_ref,
    out_buf, x_buf, z_send, z_buf, y_buf, leg_raw, leg_buf, first_buf, late_buf, last_buf, scale_buf,
    modal_buf,
    load_sem, leg_sem, x_send, x_recv, z_send_sem, z_recv, y_send, y_recv,
):
    nx, nz, ny, slots, levels, trunc, lon, block = (
        cfg[k] for k in ("nx", "nz", "ny", "slots", "levels", "trunc", "lon", "block")
    )
    lev, lat = lax.axis_index("lev"), lax.axis_index("lat")
    x, z = lat // nz, lat % nz
    y, core = lev // CORES, lev % CORES
    inner, units = lon // RADIX, trunc // RADIX
    fields = 3
    piece = 2 * fields * levels
    rows = slots * piece
    width = out_buf.shape[1]
    lats = nx * nz * 2
    total_levels = ny * CORES * levels
    flat = 2 * fields * total_levels
    bundle = 2 * nz
    bundle_z = 2 * nx

    def along_x(i):
        return {"lat": ((x + i) % nx) * nz + z}

    def along_z(i):
        return {"lat": x * nz + (z + i) % nz}

    def along_y(i):
        return {"lev": ((y + i) % ny) * CORES + core}

    partner = {"lev": y * CORES + 1 - core}

    barrier = pltpu.get_barrier_semaphore()
    peers = [along_x(i) for i in far_first(nx)] + [along_z(i) for i in far_first(nz)]
    peers += [along_y(2), along_y(ny - 2), along_y(1), along_y(ny - 1), partner]
    for peer in peers:
        pl.semaphore_signal(barrier, inc=1, device_id=peer, device_id_type=MESH)
    loads = []
    for k, (source, target) in enumerate((
        (owner_hbm, owner_ref), (hum_hbm, hum_ref), (east_hbm, east_ref), (north_hbm, north_ref),
        (table_hbm, table_ref), (modes_hbm, modes_ref), (values_hbm, values_ref),
    )):
        loads.append(pltpu.make_async_copy(source, target, load_sem.at[k]))
        loads[-1].start()
    leg_copy = pltpu.make_async_copy(
        leg_ref.at[:, pl.ds(pl.multiple_of(lev * block, 8), block), :], leg_raw, leg_sem
    )
    leg_copy.start()

    loads[0].wait()
    owner = owner_ref[...].reshape(1, trunc).astype(F32)
    owners = nx * nz
    member = owner == iota((owners, trunc), 0).astype(F32)
    before = one_hot(iota((trunc, trunc), 0) < iota((trunc, trunc), 1))
    count = dot(one_hot(member), before)
    rank = jnp.sum(jnp.where(member, count, 0.0), axis=0, keepdims=True)
    tall_slots = -(-slots // 8) * 8
    mine = (owner == lat.astype(F32)) & (rank == iota((tall_slots, trunc), 0).astype(F32))
    own_waves = jnp.sum(
        jnp.where(mine, iota((tall_slots, trunc), 1).astype(F32), 0.0), axis=1, keepdims=True
    )
    lane = iota((1, trunc), 1)
    clas = floor_div(lane, 2 * units)
    within = lane.astype(F32) - clas * (2 * units)
    second = within >= units
    unit = jnp.where(second, within - units, within)
    residue = jnp.where(second, jnp.where(clas == 0, RADIX // 2, RADIX - clas), clas)
    wave = RADIX * unit + residue
    reorder = one_hot(iota((trunc, trunc), 0).astype(F32) == wave)
    both = jnp.where(iota((16, trunc), 0) == 0, owner, jnp.where(iota((16, trunc), 0) == 1, rank, 0.0))
    both = dot(both.astype(BF16), reorder)
    owner_lane, rank_lane = both[0:1], both[1:2]

    for copy in loads[1:4]:
        copy.wait()
    humidity = hum_ref[...].astype(F32).reshape(2 * levels, lon)
    east = east_ref[...].astype(F32).reshape(2 * levels, lon)
    north = north_ref[...].astype(F32).reshape(2 * levels, lon)
    east = (east * humidity).astype(BF16).astype(F32)
    north = (north * humidity).astype(BF16).astype(F32)
    grid = jnp.concatenate([humidity, east, north], axis=0)
    real, imag = short_fourier(grid, inner)
    joined = [jnp.concatenate([r, i], axis=1) for r, i in zip(real, imag)]
    grid_rows = grid.shape[0]
    loads[4].wait()
    reals, imags = [], []
    for p in range(RADIX // 4):
        table = table_ref[p]
        if p == 0:
            left = jnp.concatenate([joined[0], joined[RADIX // 2], joined[1]], axis=0)
            limits = [units, 2 * units]
        else:
            left = jnp.concatenate([joined[2 * p], joined[2 * p + 1]], axis=0)
            limits = [2 * units]
        high = left.astype(BF16)
        low = (left - high.astype(F32)).astype(BF16)
        result = dot(high, table) + dot(low, table) + dot(high, table_ref[RADIX // 4 + p])
        column = iota((grid_rows, 8 * units), 1)
        column = jnp.where(column >= 4 * units, column - 4 * units, column)
        picked = result[len(limits) * grid_rows :]
        for k in reversed(range(len(limits))):
            picked = jnp.where(
                column < limits[k], result[k * grid_rows : (k + 1) * grid_rows], picked
            )
        reals.append(picked[:, : 4 * units])
        imags.append(picked[:, 4 * units :])
    spectrum = jnp.concatenate(
        [jnp.concatenate(reals, axis=1), jnp.concatenate(imags, axis=1)], axis=0
    ).astype(BF16)

    source = iota((piece, 2 * grid_rows), 1)
    target = iota((piece, 2 * grid_rows), 0)
    spread = []
    for t in range(2):
        pick = one_hot(2 * target + t == source)
        spread.append(dot(pick, spectrum))
    halves = []
    for t in range(2):
        pieces = [
            jnp.where(rank_lane == float(s), spread[t], 0.0) for s in range(slots)
        ] + [jnp.zeros((width - rows, trunc), F32)]
        halves.append(jnp.concatenate(pieces, axis=0))
    right = jnp.concatenate(halves, axis=1).astype(BF16)
    row = iota((2 * owners, trunc), 0).astype(F32)
    choose = jnp.concatenate(
        [
            jnp.where(2.0 * owner_lane == row, 1.0, 0.0),
            jnp.where(2.0 * owner_lane + 1.0 == row, 1.0, 0.0),
        ],
        axis=1,
    ).astype(BF16)
    out_buf[...] = dot(choose, right, (1, 1)).astype(BF16)

    pl.semaphore_wait(barrier, len(peers))

    copies = []
    for i in far_first(nx):
        to = (x + i) % nx
        copy = pltpu.make_async_remote_copy(
            src_ref=out_buf.at[pl.ds(pl.multiple_of(to * bundle, bundle), bundle)],
            dst_ref=x_buf.at[pl.ds(pl.multiple_of(x * bundle, bundle), bundle)],
            send_sem=x_send.at[i],
            recv_sem=x_recv.at[i],
            device_id=along_x(i),
            device_id_type=MESH,
        )
        copy.start()
        copies.append(copy)
    x_buf[pl.ds(pl.multiple_of(x * bundle, bundle), bundle), :] = out_buf[
        pl.ds(pl.multiple_of(x * bundle, bundle), bundle), :
    ]

    leg_copy.wait()
    arrive = iota((lats, lats), 1)
    from_z = arrive // bundle_z
    from_x = (arrive % bundle_z) // 2
    reach = one_hot(iota((lats, lats), 0) == (from_x * nz + from_z) * 2 + arrive % 2)
    leg = leg_raw[...].astype(F32).reshape(slots * block, lats).astype(BF16)
    leg = dot(leg, reach)
    degree = iota((block, lats), 0).astype(F32) + (lev * block).astype(F32)
    for s in range(slots):
        live = degree >= own_waves[s : s + 1, :]
        leg_buf[block * s : block * (s + 1), :] = jnp.where(
            live, leg[block * s : block * (s + 1)], 0.0
        )

    swap_to = iota((2 * owners, 2 * owners), 0)
    swap_from = iota((2 * owners, 2 * owners), 1)
    part_z, part_x, part_t = swap_to // bundle_z, (swap_to % bundle_z) // 2, swap_to % 2
    swap = one_hot(swap_from == part_x * bundle + part_z * 2 + part_t)

    loads[5].wait()
    loads[6].wait()
    modes = modes_ref[...]
    modes_high = modes.astype(BF16)
    modes_low = (modes - modes_high.astype(F32)).astype(BF16)
    tl = total_levels
    tile = one_hot(iota((tl, flat), 0) == (iota((tl, flat), 1) & (tl - 1)))
    column_part = iota((flat, flat), 1) // tl
    row_id = iota((flat, flat), 0)
    group = floor_div(row_id, piece)
    row_in = row_id.astype(F32) - group * piece
    row_part = floor_div(row_in, levels)
    id64 = iota((flat, tl), 0)
    group64 = floor_div(id64, piece)
    level64 = id64.astype(F32) - group64 * piece
    bases = [None] * (ny * CORES)
    for rel in range(ny):
        for side in range(CORES):
            level_group = ((y + rel) % ny) * CORES + (core if side == 0 else 1 - core)
            bases[place(rel, side)] = jnp.full(
                (piece, tl), (level_group * levels).astype(F32), F32
            )
    level64 = level64 - floor_div(level64, levels) * levels + jnp.concatenate(bases, axis=0)
    gather = one_hot(level64 == iota((flat, tl), 1).astype(F32))
    near, groups = 10, ny * CORES
    pair = 2 * tl
    late = (near + 3) * piece
    padded = late_buf.shape[0] // 2
    tile_pair = tile[:, :pair]
    same = iota((pair, pair), 0) // tl == iota((pair, pair), 1) // tl
    for k, part in enumerate((modes_high, modes_low)):
        stretched = dot(part, tile).astype(BF16)
        first = jnp.where(row_part == column_part.astype(F32), dot(gather, stretched), 0.0)
        first_buf[k] = first.astype(BF16)
        late_buf[k * padded : (k + 1) * padded, :] = jnp.concatenate(
            [first[late:], jnp.zeros((padded - flat + late, flat), F32)], axis=0
        ).astype(BF16)
        tall = dot(tile_pair, part, (0, 1)).astype(BF16)
        last_buf[k * pair : (k + 1) * pair, :] = jnp.where(
            same, dot(tall, tile_pair), 0.0
        ).astype(BF16)
    values = jnp.concatenate([values_ref[...].reshape(1, tl)] * (2 * fields), axis=1)
    number = iota((block, flat), 0).astype(F32) + (lev * block).astype(F32)
    shift = 4.0 * number * (number + 1.0) / (trunc * trunc)
    scale_buf[...] = 1.0 / (1.0 + shift * values)

    for copy in copies:
        copy.wait_recv()
    z_send[...] = dot(swap, x_buf[...]).astype(BF16)
    copies_z = []
    for i in far_first(nz):
        to = (z + i) % nz
        copy = pltpu.make_async_remote_copy(
            src_ref=z_send.at[pl.ds(pl.multiple_of(to * bundle_z, bundle_z), bundle_z)],
            dst_ref=z_buf.at[pl.ds(pl.multiple_of(z * bundle_z, bundle_z), bundle_z)],
            send_sem=z_send_sem.at[i],
            recv_sem=z_recv.at[i],
            device_id=along_z(i),
            device_id_type=MESH,
        )
        copy.start()
        copies_z.append(copy)
    z_buf[pl.ds(pl.multiple_of(z * bundle_z, bundle_z), bundle_z), :] = z_send[
        pl.ds(pl.multiple_of(z * bundle_z, bundle_z), bundle_z), :
    ]

    for copy in copies_z:
        copy.wait_recv()
    own = z_buf[...].astype(F32).T
    y_buf[place(0, 0)] = own[:rows].astype(BF16)

    pending = []
    half = cfg["half"]

    def message(k, rel, to, to_rel, side, start=0, size=rows):
        return pltpu.make_async_remote_copy(
            src_ref=y_buf.at[place(rel, 0), pl.ds(start, size)],
            dst_ref=y_buf.at[place(to_rel, side), pl.ds(start, size)],
            send_sem=y_send.at[k],
            recv_sem=y_recv.at[k],
            device_id=to,
            device_id_type=MESH,
        )

    def send(k, rel, step, start=0, size=rows):
        copy = message(k, rel, along_y(step % ny), (rel - step) % ny, 0, start, size)
        copy.start()
        return copy

    def relay(*args):
        pending.append(send(*args))

    def hand(k, rel, start=0, size=rows):
        copy = message(k, rel, partner, rel, 1, start, size)
        copy.start()
        pending.append(copy)

    def arrive_from(k, rel, side, start=0, size=rows):
        view = y_buf.at[place(rel, side), pl.ds(start, size)]
        pltpu.make_async_remote_copy(
            src_ref=view, dst_ref=view, send_sem=y_send.at[k], recv_sem=y_recv.at[k],
            device_id=partner, device_id_type=MESH,
        ).wait_recv()

    lower, upper = (0, half), (half, rows - half)
    step = half // 2
    parts = [(0, step), (step, half - step), (half, step), (half + step, rows - half - step)]
    below, above = ny - 2, 2
    rise, fall = (0, 1, 2, 3), (2, 3, 0, 1)
    for i, j in zip(rise, fall):
        relay(i, 0, 2, *parts[i])
        relay(4 + j, 0, -2, *parts[j])
    relay(8, 0, 1)
    relay(9, 0, -1)
    hand(22, 0)
    for i, j in zip(rise, fall):
        arrive_from(i, below, 0, *parts[i])
        if i < 2:
            relay(10 + i, below, 2, *parts[i])
        relay(14 + i, below, 1, *parts[i])
        arrive_from(4 + j, above, 0, *parts[j])
        if j >= 2:
            relay(10 + j, above, -2, *parts[j])
        relay(18 + j, above, -1, *parts[j])
    hand(23, below)
    hand(24, above)
    arrive_from(8, ny - 1, 0)
    hand(25, ny - 1)
    arrive_from(9, 1, 0)
    hand(26, 1)
    for k, rel in ((22, 0), (23, below), (24, above), (25, ny - 1), (26, 1)):
        arrive_from(k, rel, 1)

    def project(first, last, padding):
        pieces = []
        for s in range(slots):
            blocks = [y_buf[g, piece * s : piece * (s + 1), :] for g in range(first, last)]
            if padding:
                blocks.append(jnp.zeros((padding, lats), BF16))
            left = leg_buf[block * s : block * (s + 1), :].astype(BF16)
            pieces.append(dot(left, jnp.concatenate(blocks, axis=0), (1, 1)))
        return jnp.concatenate(pieces, axis=0).astype(BF16)

    def modal_part(first, last):
        projected = project(first, last, 0)
        span = slice(first * piece, last * piece)
        return dot(projected, first_buf[0, span, :]) + dot(projected, first_buf[1, span, :])

    modal_buf[...] = modal_part(0, near)
    for i in (0, 1):
        arrive_from(14 + i, ny - 3, 0, *parts[i])
    hand(28, ny - 3, *lower)
    for i in (2, 3):
        arrive_from(18 + i, 3, 0, *parts[i])
    hand(29, 3, *upper)
    for i in range(4):
        arrive_from(10 + i, 4, 0, *parts[i])
    hand(27, 4)
    for i in (2, 3):
        arrive_from(14 + i, ny - 3, 0, *parts[i])
    hand(30, ny - 3, *upper)
    for i in (0, 1):
        arrive_from(18 + i, 3, 0, *parts[i])
    hand(31, 3, *lower)
    modal_buf[...] += modal_part(near, near + 3)
    arrive_from(27, 4, 1)
    arrive_from(28, ny - 3, 1, *lower)
    arrive_from(29, 3, 1, *upper)
    arrive_from(30, ny - 3, 1, *upper)
    arrive_from(31, 3, 1, *lower)
    projected = project(near + 3, groups, padded - flat + late)
    modal = modal_buf[...] + dot(jnp.concatenate([projected, projected], axis=1), late_buf[...])
    scale = jnp.concatenate([scale_buf[...]] * slots, axis=0)
    modal = (modal * scale).astype(BF16)
    solved = []
    for j in range(flat // pair):
        part = modal[:, j * pair : (j + 1) * pair]
        solved.append(dot(jnp.concatenate([part, part], axis=1), last_buf[...]))
    solved = jnp.concatenate(solved, axis=1)
    out_ref[...] = solved.reshape(slots, block, flat)

    for copy in copies + copies_z + pending:
        copy.wait_send()


def build(nx, nz, ny, slots, levels, trunc, lon, half, width):
    block = trunc // (ny * CORES)
    rows = slots * 6 * levels
    total_levels = levels * ny * CORES
    flat = 6 * total_levels
    lats = nx * nz * 2
    inner, units = lon // RADIX, trunc // RADIX
    cfg = dict(
        nx=nx, nz=nz, ny=ny, slots=slots, levels=levels, trunc=trunc, lon=lon, block=block,
        half=half,
    )
    dma = pltpu.SemaphoreType.DMA
    hbm = pl.BlockSpec(memory_space=pltpu.HBM)
    return pl.pallas_call(
        functools.partial(kernel, cfg),
        out_shape=jax.ShapeDtypeStruct((slots, block, flat), F32),
        in_specs=[hbm] * 8,
        out_specs=pl.BlockSpec(memory_space=pltpu.VMEM),
        scratch_shapes=[
            pltpu.VMEM((levels, 2, lon), BF16),
            pltpu.VMEM((levels, 2, lon), BF16),
            pltpu.VMEM((levels, 2, lon), BF16),
            pltpu.VMEM((trunc,), jnp.int32),
            pltpu.VMEM((total_levels, total_levels), F32),
            pltpu.VMEM((total_levels,), F32),
            pltpu.VMEM((RADIX // 2, 2 * inner, 8 * units), BF16),
            pltpu.VMEM((lats, width), BF16),
            pltpu.VMEM((lats, width), BF16),
            pltpu.VMEM((lats, width), BF16),
            pltpu.VMEM((lats, width), BF16),
            pltpu.VMEM((ny * CORES, rows, lats), BF16),
            pltpu.VMEM((slots, block, lats), BF16),
            pltpu.VMEM((slots * block, lats), F32),
            pltpu.VMEM((2, flat, flat), BF16),
            pltpu.VMEM((2 * (-(-18 * levels // 128) * 128), flat), BF16),
            pltpu.VMEM((4 * total_levels, 2 * total_levels), BF16),
            pltpu.VMEM((block, flat), F32),
            pltpu.VMEM((slots * block, flat), F32),
            dma((7,)), dma, dma((nx,)), dma((nx,)), dma((nz,)), dma((nz,)), dma((32,)), dma((32,)),
        ],
        compiler_params=pltpu.CompilerParams(
            collective_id=0, has_side_effects=True, vmem_limit_bytes=VMEM_LIMIT
        ),
    )


def body(humidity, wind_east, wind_north, legendre, owner, vertical_modes, mode_values):
    trunc = owner.shape[0]
    levels, pair, lon = humidity.shape
    owners = lax.axis_size("lat")
    nx, nz = split_lat(owners)
    ny = lax.axis_size("lev") // CORES
    slots = legendre.shape[0]
    rows = slots * 6 * levels
    half = -(-rows // 32) * 16
    width = -(-rows // 128) * 128
    table = fourier_table(lon, trunc // RADIX)
    high = table.astype(BF16)
    table = jnp.asarray(np.concatenate([high, (table - high.astype(np.float64)).astype(BF16)]))
    call = build(nx, nz, ny, slots, levels, trunc, lon, half, width)
    operands = [humidity, wind_east, wind_north, legendre, owner, vertical_modes, mode_values, table]
    return call(*[pltpu.with_memory_space_constraint(v, pltpu.HBM) for v in operands])


def solution(mesh):
    return jax.shard_map(
        body,
        mesh=mesh,
        in_specs=(
            P("lev", "lat", None),
            P("lev", "lat", None),
            P("lev", "lat", None),
            P("lat", None, None),
            P(),
            P(),
            P(),
        ),
        out_specs=P("lat", "lev", None),
        check_vma=False,
    )
```
